128 devices in a mesh: dp: 16 (over y, x), row: 4 (over z), col: 2 (over core).
Axes of the slice: x: 4, y: 4, z: 4, core: 2. Of those that a mesh axis runs over, the one named last changes fastest.
Arguments:
- tokens: bfloat16 [4096, 4096], P(('dp', 'col'), 'row'), may hold values from -6 to 6
- w_up: bfloat16 [4096, 16384], P('row', 'col'), may hold values from -0.09375 to 0.09375
- w_down: bfloat16 [4096, 16384], P('row', 'col'), may hold values from -0.046875 to 0.046875
- cotangent: bfloat16 [4096, 4096], P(('dp', 'col'), 'row'), may hold values from -6 to 6
Outputs:
- output: bfloat16 [4096, 4096], P(('dp', 'col'), 'row')
- input_grad: bfloat16 [4096, 4096], P(('dp', 'col'), 'row')
- up_grad: float32 [4096, 16384], P('row', ('col', 'dp'))
- down_grad: float32 [4096, 16384], P('row', ('col', 'dp'))
The draws below stay inside these ranges and needn't reach their ends.
All inputs are finite; a program needn't handle non-finite values.
Results may differ from the reference program's by a relative error of at most 0.018.
Values may be sent and summed in bfloat16 or wider, within the bound.
A program may use at most 192 MiB of HBM per device.

```python
import jax
import jax.numpy as jnp
from jax import lax

D = 4096
F = 16384
TOKENS = 4096
N_ROW = 4


def block_scale(own_key, shape, pieces, smallest, top_value):
    def one(axis_at, shards_of):
        draws = jax.random.uniform(jax.random.fold_in(jax.random.fold_in(own_key, 6), axis_at), (shards_of,), jnp.float32, smallest / len(pieces), top_value / len(pieces))
        return jnp.repeat(jnp.exp(draws), shape[axis_at] // shards_of).reshape((-1,) + (1,) * (len(shape) - axis_at - 1))

    factor_of = one(*pieces[0])
    for cut in pieces[1:]:
        factor_of = factor_of * one(*cut)
    return factor_of


def normal_values(rng, dims, deviation, limit, shards=(), kind=jnp.bfloat16):
    result = deviation * jax.random.normal(rng, dims, jnp.float32)
    if shards:
        result = result * block_scale(rng, dims, shards, -0.22, 0.18)
    return jnp.clip(result, -limit, limit).astype(kind)


def setup_inputs(seed: int = 0) -> dict:
    seeds = jax.random.split(jax.random.key(seed), 5)
    return {
        "tokens": normal_values(seeds[0], (TOKENS, D), 1.0, 6.0, ((0, 32), (1, 4))),
        "w_up": normal_values(seeds[1], (D, F), D ** -0.5, 0.09375, ((0, 4), (1, 2))),
        "w_down": normal_values(seeds[2], (D, F), F ** -0.5, 0.046875, ((0, 4), (1, 2))),
        "cotangent": normal_values(seeds[3], (TOKENS, D), 1.0, 6.0, ((0, 32), (1, 4))),
    }


gelu_coef = 0.7978845608
cubic_coef = 0.044715


def rounded(matrix):
    return lax.optimization_barrier(matrix.astype(jnp.bfloat16)).astype(jnp.float32)


def gelu_pair(hidden):
    tangent = jnp.tanh(gelu_coef * (hidden + cubic_coef * hidden * hidden * hidden))
    activated = 0.5 * hidden * (1.0 + tangent)
    derivative = 0.5 * (1.0 + tangent) + 0.5 * hidden * (1.0 - tangent * tangent) * gelu_coef * (1.0 + 3.0 * cubic_coef * hidden * hidden)
    return activated, derivative


def reference(tokens, w_up, w_down, cotangent):
    width_block = D // N_ROW
    hidden = jnp.zeros((tokens.shape[0], F), jnp.float32)
    back = jnp.zeros((tokens.shape[0], F), jnp.float32)
    for index_row in range(N_ROW):
        first = index_row * width_block
        hidden = hidden + rounded(jnp.dot(tokens[:, first:first + width_block], w_up[first:first + width_block], preferred_element_type=jnp.float32))
        back = back + rounded(jnp.dot(cotangent[:, first:first + width_block], w_down[first:first + width_block], preferred_element_type=jnp.float32))
    activated, derivative = gelu_pair(hidden)
    activated = activated.astype(jnp.bfloat16)
    output = jnp.dot(activated, w_down.T, preferred_element_type=jnp.float32).astype(jnp.bfloat16)
    hidden_grad = (back * derivative).astype(jnp.bfloat16)
    input_grad = jnp.dot(hidden_grad, w_up.T, preferred_element_type=jnp.float32).astype(jnp.bfloat16)
    grad_scale = float(TOKENS) ** -0.5
    up_grad = grad_scale * jnp.dot(tokens.T, hidden_grad, preferred_element_type=jnp.float32)
    down_grad = grad_scale * jnp.dot(cotangent.T, activated, preferred_element_type=jnp.float32)
    return output, input_grad, up_grad, down_grad
```

```python
import jax
import jax.numpy as jnp
from jax import lax
from jax.experimental import pallas as pl
from jax.experimental.pallas import tpu as pltpu
from jax.sharding import PartitionSpec as P

MESH = pl.DeviceIdType.MESH
bf16 = jnp.bfloat16
f32 = jnp.float32
gelu_coef = 0.7978845608
cubic_coef = 0.044715

SHARD = 128
WIDE = 1024
SLICE = 512
TOK = 16 * SHARD
HID = 2 * SLICE
CHUNKS = ((0, 256), (256, 256), (512, 512))


def mm(left, right, dim_left, dim_right):
    return lax.dot_general(
        left, right, (((dim_left,), (dim_right,)), ((), ())), preferred_element_type=f32
    )


def kernel(
    tok, cot, wup, wdn, oo, ga, gb,
    xv, wv, pb, pr, sb, sr, gv, ob, r1, r2, fb, gs,
    k_xin, k_x, k_ws, k_w, k_ag, k_bs, k_b, k_bs2, k_b2, k_ss, k_s, k_r1s, k_r1, k_r2s, k_r2, k_gs, k_g, k_os, k_o,
):
    dp, z, c = lax.axis_index("dp"), lax.axis_index("row"), lax.axis_index("col")
    y, x = lax.div(dp, 4), lax.rem(dp, 4)
    half, i = lax.div(z, 2), lax.rem(z, 2)
    za, zb = z + 1 - 2 * i, 3 - z
    tau = lax.rem(lax.div(z + 1, 2), 2)

    def remote(src, dst, send, recv, dev):
        return pltpu.make_async_remote_copy(
            src_ref=src, dst_ref=dst, send_sem=send, recv_sem=recv, device_id=dev, device_id_type=MESH
        )

    def arrived(dst, sem):
        pltpu.make_async_copy(dst, dst, sem).wait()

    def xy(o1, o2):
        px = lax.rem(x + o1 * (1 - c) + o2 * c, 4)
        py = lax.rem(y + o1 * c + o2 * (1 - c), 4)
        return px, py

    def dev(o1, o2):
        px, py = xy(o1, o2)
        return {"dp": py * 4 + px, "row": z, "col": c}

    def slot(o1, o2):
        px, py = xy(o1, o2)
        return lax.rem(px - py + 4, 4) * 4 + py

    def rows(s):
        return pl.ds(pl.multiple_of(s * SHARD, SHARD), SHARD)

    def at_z(zz, cc):
        return {"dp": dp, "row": zz, "col": cc}

    sends = []

    def put(local, src, dst, send, recv, to):
        copy = remote(src, dst, send, recv, to)
        if local is None:
            copy.start()
        else:
            @pl.when(local)
            def _():
                pltpu.make_async_copy(src, dst, recv).start()

            @pl.when(jnp.logical_not(local))
            def _():
                copy.start()
        sends.append((local, copy))

    barrier = pltpu.get_barrier_semaphore()
    peers = [at_z(za, 0), at_z(za, 1), at_z(zb, c), at_z(z, 1 - c)]
    peers += [dev(o, 0) for o in (1, 2, 3)] + [dev(0, o) for o in (1, 2, 3)]
    for peer in peers:
        pl.semaphore_signal(barrier, inc=1, device_id=peer, device_id_type=MESH)
    pl.semaphore_wait(barrier, len(peers))

    own = slot(0, 0)
    here = c == tau
    zx = z * (1 - lax.rem(c + tau, 2)) + za * lax.rem(c + tau, 2)
    for role, src in ((0, tok), (1, cot)):
        put(
            jnp.logical_and(here, c == role), src, xv.at[i, rows(own), :],
            k_xin.at[role], k_x.at[i, own], at_z(zx, role),
        )
    for k, (f0, fw) in enumerate(CHUNKS):
        n = fw // 2
        cols = pl.ds(pl.multiple_of(dp * SLICE + f0 // 2, 128), n)
        into = pl.ds(pl.multiple_of(f0 + c * n, 128), n)
        for rel, zz in ((1, za), (0, z)):
            for role, src in ((0, wup), (1, wdn)):
                put(
                    (c == role) if rel == 0 else None, src.at[:, cols], wv.at[i, :, into],
                    k_ws.at[k, rel, role], k_w.at[k, i, c], at_z(zz, role),
                )

    def weights(k):
        f0, fw = CHUNKS[k]
        n = fw // 2
        for db in range(2):
            for cc in range(2):
                arrived(wv.at[db, :, pl.ds(f0 + cc * n, n)], k_w.at[k, db, cc])

    count = [0]

    def shard_to(db, s, to):
        part = xv.at[db, rows(s), :]
        put(None, part, part, k_ag.at[count[0]], k_x.at[db, s], to)
        count[0] += 1

    def shard_in(db, s):
        arrived(xv.at[db, rows(s), :], k_x.at[db, s])

    def hidden(row0, m, f0, fw, step):
        r = pl.ds(row0, m)
        for n0 in range(f0, f0 + fw, step):
            cs = pl.ds(n0, step)
            part = mm(xv[0, r, :], wv[0, :, cs], 1, 0) + mm(xv[1, r, :], wv[1, :, cs], 1, 0)
            pb[r, cs] = part.astype(bf16)

    def hidden_line(o2, k):
        f0, fw = CHUNKS[k]

        @pl.loop(0, 4)
        def _(o1):
            hidden(pl.multiple_of(slot(o1, o2) * SHARD, SHARD), SHARD, f0, fw, fw)

        for o1 in range(4):
            s = slot(o1, o2)
            put(
                None, pb.at[rows(s), pl.ds(f0, fw)], pr.at[rows(s), pl.ds(f0, fw)],
                k_bs.at[k, s], k_b.at[k, s], at_z(zb, c),
            )

    def across(o1, from_):
        s = slot(o1, from_)
        for db in range(2):
            shard_in(db, s)
            if (from_, db) in ((3, 0), (1, 1)):
                shard_to(db, s, dev(0, 4 - from_))

    for db in range(2):
        shard_in(db, own)
        for to in (dev(1, 0), dev(3, 0), dev(0, 1), dev(0, 3)):
            shard_to(db, own, to)
    for o1 in (3, 1):
        s = slot(o1, 0)
        for db in range(2):
            shard_in(db, s)
            if (o1, db) in ((3, 0), (1, 1)):
                shard_to(db, s, dev(4 - o1, 0))
            for to in (dev(0, 1), dev(0, 3)):
                shard_to(db, s, to)
    across(0, 3)
    across(0, 1)
    for db in range(2):
        shard_in(db, slot(2, 0))
        for to in (dev(0, 1), dev(0, 3)):
            shard_to(db, slot(2, 0), to)
    weights(0)
    hidden_line(0, 0)
    for o1 in (3, 1):
        across(o1, 3)
        across(o1, 1)
    weights(1)
    hidden_line(0, 1)
    across(2, 3)
    across(2, 1)
    for o2 in (3, 1):
        hidden_line(o2, 0)
        hidden_line(o2, 1)
    for o1 in (0, 3, 1, 2):
        for db in range(2):
            shard_in(db, slot(o1, 2))
    hidden_line(2, 0)
    hidden_line(2, 1)
    weights(2)
    f2, w2 = CHUNKS[2]
    GROUP = 4 * SHARD
    for g in range(4):
        r = pl.ds(g * GROUP, GROUP)
        hidden(g * GROUP, GROUP, f2, w2, w2)
        put(None, pb.at[r, pl.ds(f2, w2)], pr.at[r, pl.ds(f2, w2)], k_bs2.at[g], k_b2.at[g], at_z(zb, c))

    def tiles(g, f0, body):
        @pl.loop(0, GROUP // 32)
        def _(a):
            for n0 in range(f0, f0 + SLICE, 256):
                body(pl.ds(pl.multiple_of(g * GROUP + a * 32, 32), 32), pl.ds(n0, 256))

    def combine(p, g):
        f0 = p * SLICE

        def body(r, cs):
            sb[r, cs] = (pb[r, cs].astype(f32) + pr[r, cs].astype(f32)).astype(bf16)

        tiles(g, f0, body)
        part = (pl.ds(g * GROUP, GROUP), pl.ds(f0, SLICE))
        put(None, sb.at[part], sr.at[part], k_ss.at[p, g], k_s.at[p, g], at_z(z, 1 - c))

    def activate(p, g):
        f0 = p * SLICE
        part = (pl.ds(g * GROUP, GROUP), pl.ds(f0, SLICE))
        arrived(sr.at[part], k_s.at[p, g])

        def grad(r, cs):
            hid, back = sb[r, cs].astype(f32), sr[r, cs].astype(f32)
            square = hid * hid
            t = jnp.tanh(gelu_coef * (hid + cubic_coef * square * hid))
            slope = 0.5 * (1.0 + t) + 0.5 * hid * (1.0 - t * t) * gelu_coef * (1.0 + 3.0 * cubic_coef * square)
            gv[r, cs] = (back * slope).astype(bf16)

        def act(r, cs):
            hid = sr[r, cs].astype(f32)
            t = jnp.tanh(gelu_coef * (hid + cubic_coef * hid * hid * hid))
            gv[r, cs] = (0.5 * hid * (1.0 + t)).astype(bf16)

        @pl.when(c == 0)
        def _():
            tiles(g, f0, grad)

        @pl.when(c == 1)
        def _():
            tiles(g, f0, act)

    def weight_grads(p):
        cs = pl.ds(p * SLICE, SLICE)

        @pl.loop(0, 2)
        def _(db):
            @pl.loop(0, WIDE // 256)
            def _(j):
                r = pl.ds(pl.multiple_of(j * 256, 256), 256)
                gs[db, r, cs] = mm(xv[db, :, r], gv[:, cs], 0, 0).astype(bf16)

        for k, (f0, fw) in enumerate(CHUNKS):
            if f0 // SLICE != p:
                continue
            n = fw // 2
            for rel, zz, db, out in ((1, za, 1 - i, gb), (0, z, i, ga)):
                for cc in range(2):
                    put(
                        (c == cc) if rel == 0 else None,
                        gs.at[db, :, pl.ds(f0 + cc * n, n)], out.at[c, :, pl.ds(f0 // 2, n)],
                        k_gs.at[k, rel, cc], k_g.at[k, rel, c], at_z(zz, cc),
                    )

    for g in range(4):
        for s in range(4 * g, 4 * g + 4):
            for k in range(2):
                f0, fw = CHUNKS[k]
                arrived(pr.at[rows(s), pl.ds(f0, fw)], k_b.at[k, s])
        combine(0, g)
        if g:
            activate(0, g - 1)
    activate(0, 3)
    weight_grads(0)

    def line_slot(g, o2):
        return 4 * g + lax.rem((1 - c) * (y + o2) + c * (x + o2 - g + 4), 4)

    def reduce_line(g):
        s = line_slot(g, 0)
        for o in range(3):
            arrived(r1.at[g, o], k_r1.at[g, o])

        @pl.loop(0, SHARD // 16)
        def _(a):
            src = pl.ds(pl.multiple_of(a * 16, 16), 16)
            dst = pl.ds(pl.multiple_of(s * SHARD + a * 16, 16), 16)
            for db in range(2):
                total = ob[db, dst, :].astype(f32)
                for o in range(3):
                    total = total + r1[g, o, db, src, :].astype(f32)
                ob[db, dst, :] = total.astype(bf16)

        o1 = lax.rem((1 - c) * (g + y - x + 4) + c * (x - g - y + 8), 4)
        slot2 = lax.rem(o1 + 3, 4)

        @pl.when(o1 != 0)
        def _():
            remote(
                ob.at[:, rows(s), :], r2.at[slot2], k_r2s.at[slot2], k_r2.at[slot2], dev(o1, 0)
            ).start()

    for g in range(4):
        r = pl.ds(g * GROUP, GROUP)
        arrived(pr.at[r, pl.ds(f2, w2)], k_b2.at[g])
        combine(1, g)
        activate(1, g)

        @pl.loop(0, 2)
        def _(db):
            @pl.loop(0, 2)
            def _(j):
                ds = pl.ds(pl.multiple_of(j * 512, 512), 512)
                ob[db, r, ds] = mm(gv[r, :], wv[db, ds, :], 1, 1).astype(bf16)

        for o in (2, 1, 3):
            s = line_slot(g, o)
            put(None, ob.at[:, rows(s), :], r1.at[g, o - 1], k_r1s.at[g, o - 1], k_r1.at[g, o - 1], dev(0, o))
        if g:
            reduce_line(g - 1)
    weight_grads(1)
    reduce_line(3)
    for o in range(3):
        arrived(r2.at[o], k_r2.at[o])

    @pl.loop(0, SHARD // 16)
    def _(a):
        src = pl.ds(pl.multiple_of(a * 16, 16), 16)
        dst = pl.ds(pl.multiple_of(own * SHARD + a * 16, 16), 16)
        for db in range(2):
            total = ob[db, dst, :].astype(f32)
            for o in range(3):
                total = total + r2[o, db, src, :].astype(f32)
            fb[db, src, :] = total.astype(bf16)

    for rel, zz, db in ((1, za, 1 - i), (0, z, i)):
        put(
            (tau == c) if rel == 0 else None, fb.at[db], oo.at[c], k_os.at[rel], k_o.at[c], at_z(zz, tau)
        )

    for role in range(2):
        arrived(oo.at[role], k_o.at[role])
        for k, (f0, fw) in enumerate(CHUNKS):
            for rel, out in ((0, ga), (1, gb)):
                arrived(out.at[role, :, pl.ds(f0 // 2, fw // 2)], k_g.at[k, rel, role])
    for o in range(3):
        remote(ob.at[:, pl.ds(0, SHARD), :], r2.at[o], k_r2s.at[o], k_r2.at[o], dev(1, 0)).wait_send()
    for local, copy in sends:
        if local is None:
            copy.wait_send()
        else:
            @pl.when(jnp.logical_not(local))
            def _():
                copy.wait_send()


def body(tokens, w_up, w_down, cotangent):
    batch_total = tokens.shape[0] * lax.axis_size("col") * lax.axis_size("dp")
    grad_scale = float(batch_total) ** (-0.5)
    dma = pltpu.SemaphoreType.DMA
    anywhere = pl.BlockSpec(memory_space=pl.ANY)
    oo, ga, gb = pl.pallas_call(
        kernel,
        out_shape=(
            jax.ShapeDtypeStruct((2, SHARD, WIDE), bf16),
            jax.ShapeDtypeStruct((2, WIDE, SLICE), bf16),
            jax.ShapeDtypeStruct((2, WIDE, SLICE), bf16),
        ),
        in_specs=[anywhere] * 4,
        out_specs=(anywhere,) * 3,
        scratch_shapes=[
            pltpu.VMEM((2, TOK, WIDE), bf16),
            pltpu.VMEM((2, WIDE, HID), bf16),
            pltpu.VMEM((TOK, HID), bf16),
            pltpu.VMEM((TOK, HID), bf16),
            pltpu.VMEM((TOK, HID), bf16),
            pltpu.VMEM((TOK, HID), bf16),
            pltpu.VMEM((TOK, HID), bf16),
            pltpu.VMEM((2, TOK, WIDE), bf16),
            pltpu.VMEM((4, 3, 2, SHARD, WIDE), bf16),
            pltpu.VMEM((3, 2, SHARD, WIDE), bf16),
            pltpu.VMEM((2, SHARD, WIDE), bf16),
            pltpu.VMEM((2, WIDE, HID), bf16),
            dma((2,)), dma((2, 16)),
            dma((3, 2, 2)), dma((3, 2, 2)),
            dma((30,)),
            dma((2, 16)), dma((2, 16)), dma((4,)), dma((4,)),
            dma((2, 4)), dma((2, 4)),
            dma((4, 3)), dma((4, 3)), dma((3,)), dma((3,)),
            dma((3, 2, 2)), dma((3, 2, 2)),
            dma((2,)), dma((2,)),
        ],
        compiler_params=pltpu.CompilerParams(
            collective_id=0, has_side_effects=True, vmem_limit_bytes=63 << 20
        ),
        name="ffn",
    )(tokens, cotangent, w_up, w_down)
    up_grad = grad_scale * (ga[0].astype(f32) + gb[0].astype(f32))
    down_grad = grad_scale * (ga[1].astype(f32) + gb[1].astype(f32))
    return (oo[1], oo[0], up_grad, down_grad)


def solution(mesh):
    placed = (P(("dp", "col"), "row"), P("row", "col"), P("row", "col"), P(("dp", "col"), "row"))
    return jax.shard_map(
        body,
        mesh=mesh,
        in_specs=placed,
        out_specs=(
            P(("dp", "col"), "row"),
            P(("dp", "col"), "row"),
            P("row", ("col", "dp")),
            P("row", ("col", "dp")),
        ),
        check_vma=False,
    )
```

```python
import jax
import jax.numpy as jnp
from jax import lax
from jax.experimental import pallas as pl
from jax.experimental.pallas import tpu as pltpu
from jax.sharding import PartitionSpec as P

MESH = pl.DeviceIdType.MESH
bf16 = jnp.bfloat16
f32 = jnp.float32
gelu_coef = 0.7978845608
cubic_coef = 0.044715

SHARD = 128
WIDE = 1024
SLICE = 512
TOK = 16 * SHARD
HID = 2 * SLICE
UNIT = 128
CHUNKS = ((0, 2), (2, 2), (4, 1), (5, 3))
EARLY = 5 * UNIT
PASSES = ((0, EARLY), (EARLY, HID - EARLY))
PIECE = SHARD // 4
GROUP = 16 * PIECE


def mm(left, right, dim_left, dim_right):
    return lax.dot_general(
        left, right, (((dim_left,), (dim_right,)), ((), ())), preferred_element_type=f32
    )


def kernel(
    tok, cot, wup, wdn, oo, ga, gb,
    xv, wv, pb, pr, sb, sr, gv, ob, r1, rl, r2, fb, gs, acc,
    k_xin, k_x, k_ws, k_w, k_ag, k_bs, k_b, k_bs2, k_b2, k_ss, k_s,
    k_r1s, k_r1, k_rls, k_rl, k_r2s, k_r2, k_gs, k_g, k_os, k_o,
):
    dp, z, c = lax.axis_index("dp"), lax.axis_index("row"), lax.axis_index("col")
    y, x = lax.div(dp, 4), lax.rem(dp, 4)
    half, i = lax.div(z, 2), lax.rem(z, 2)
    za, zb = z + 1 - 2 * i, 3 - z
    tau = lax.rem(lax.div(z + 1, 2), 2)

    def remote(src, dst, send, recv, dev):
        return pltpu.make_async_remote_copy(
            src_ref=src, dst_ref=dst, send_sem=send, recv_sem=recv, device_id=dev, device_id_type=MESH
        )

    def arrived(dst, sem):
        pltpu.make_async_copy(dst, dst, sem).wait()

    a1, a2 = x * (1 - c) + y * c, y * (1 - c) + x * c

    def place(o1, o2):
        return lax.rem(a2 + o2, 4), lax.rem(a1 + o1, 4)

    def number(p):
        return p[0] * 4 + p[1]

    def dev(o1, o2):
        p2, p1 = place(o1, o2)
        return {"dp": (p1 * c + p2 * (1 - c)) * 4 + p1 * (1 - c) + p2 * c, "row": z, "col": c}

    def at_z(zz, cc):
        return {"dp": dp, "row": zz, "col": cc}

    sends = []

    def put(local, src, dst, send, recv, to):
        copy = remote(src, dst, send, recv, to)
        if local is None:
            copy.start()
        else:
            @pl.when(local)
            def _():
                pltpu.make_async_copy(src, dst, recv).start()

            @pl.when(jnp.logical_not(local))
            def _():
                copy.start()
        sends.append((local, copy))

    barrier = pltpu.get_barrier_semaphore()
    peers = [at_z(za, 0), at_z(za, 1), at_z(zb, c), at_z(z, 1 - c)]
    peers += [dev(o, 0) for o in (1, 2, 3)] + [dev(0, o) for o in (1, 2, 3)]
    for peer in peers:
        pl.semaphore_signal(barrier, inc=1, device_id=peer, device_id_type=MESH)
    pl.semaphore_wait(barrier, len(peers))

    own = place(0, 0)
    here = c == tau
    zx = z * (1 - lax.rem(c + tau, 2)) + za * lax.rem(c + tau, 2)
    for role, src, p in ((0, tok, (y, x)), (1, cot, (x, y))):
        put(
            jnp.logical_and(here, c == role), src, xv.at[i, :, p[0], p[1]],
            k_xin.at[role], k_x.at[i, number(p)], at_z(zx, role),
        )
    for m in range(4):
        u = 2 * m + c
        cols = pl.ds(pl.multiple_of(dp * SLICE + m * UNIT, UNIT), UNIT)
        into = pl.ds(pl.multiple_of(u * UNIT, UNIT), UNIT)
        for rel, zz in ((1, za), (0, z)):
            for role, src in ((0, wup), (1, wdn)):
                put(
                    (c == role) if rel == 0 else None, src.at[:, cols], wv.at[i, :, into],
                    k_ws.at[m, rel, role], k_w.at[u, i], at_z(zz, role),
                )

    def weights(k):
        u0, n = CHUNKS[k]
        for u in range(u0, u0 + n):
            for db in range(2):
                arrived(wv.at[db, :, pl.ds(u * UNIT, UNIT)], k_w.at[u, db])

    count = [0]

    def shard_to(db, p, to):
        part = xv.at[db, :, p[0], p[1]]
        put(None, part, part, k_ag.at[count[0]], k_x.at[db, number(p)], to)
        count[0] += 1

    def shard_in(db, p):
        arrived(xv.at[db, :, p[0], p[1]], k_x.at[db, number(p)])

    def hidden(part, m, shape, f0, fw):
        cs = pl.ds(f0, fw)
        total = [mm(xv[(db, *part)].reshape(m, WIDE), wv[db, :, cs], 1, 0) for db in range(2)]
        pb[(*part, slice(None), cs)] = (total[0] + total[1]).astype(bf16).reshape(*shape, PIECE, fw)

    def hidden_line(o1, o2s, chunks):
        for k in chunks:
            f0, fw = CHUNKS[k][0] * UNIT, CHUNKS[k][1] * UNIT

            @pl.loop(0, len(o2s))
            def _(j):
                p = place(o1, lax.rem(j + o2s[0], 4))
                hidden((slice(None), p[0], p[1]), SHARD, (4,), f0, fw)

            for o2 in o2s:
                p = place(o1, o2)
                at = (slice(None), p[0], p[1], slice(None), pl.ds(f0, fw))
                put(None, pb.at[at], pr.at[at], k_bs.at[k, number(p)], k_b.at[k, number(p)], at_z(zb, c))

    halves = (i, 1 - i)

    def across(o1, o2):
        p = place(o1, o2)
        for way, db in enumerate(halves):
            shard_in(db, p)
            if (o2, way) in ((3, 0), (1, 1)):
                shard_to(db, p, dev(0, 4 - o2))

    near, far, full = (3, 0, 1), (2,), (3, 0, 1, 2)
    for db in halves:
        shard_in(db, own)
        for to in (dev(1, 0), dev(3, 0), dev(0, 1), dev(0, 3)):
            shard_to(db, own, to)
    for o1 in (3, 1):
        p = place(o1, 0)
        for way, db in enumerate(halves):
            shard_in(db, p)
            if (o1, way) in ((3, 0), (1, 1)):
                shard_to(db, p, dev(4 - o1, 0))
            for to in (dev(0, 1), dev(0, 3)):
                shard_to(db, p, to)
    across(0, 3)
    across(0, 1)
    for db in halves:
        shard_in(db, place(2, 0))
        for to in (dev(0, 1), dev(0, 3)):
            shard_to(db, place(2, 0), to)
    weights(0)
    hidden_line(0, near, (0,))
    across(3, 3)
    across(3, 1)
    hidden_line(3, near, (0,))
    across(0, 2)
    hidden_line(0, far, (0,))
    weights(1)
    hidden_line(0, full, (1,))
    hidden_line(3, near, (1,))
    across(1, 3)
    across(1, 1)
    hidden_line(1, near, (0, 1))
    across(3, 2)
    hidden_line(3, far, (0, 1))
    weights(2)
    hidden_line(0, full, (2,))
    hidden_line(3, full, (2,))
    hidden_line(1, near, (2,))
    across(2, 3)
    across(2, 1)
    hidden_line(2, near, (0, 1, 2))
    across(1, 2)
    hidden_line(1, far, (0, 1, 2))
    across(2, 2)
    hidden_line(2, far, (0, 1, 2))
    weights(3)
    f2, w2 = PASSES[1]

    def late(g):
        return (g, slice(None), slice(None), slice(None), pl.ds(f2, w2))

    for g in range(4):
        hidden((g, slice(None), slice(None)), GROUP, (4, 4), f2, w2)
        put(None, pb.at[late(g)], pr.at[late(g)], k_bs2.at[g], k_b2.at[g], at_z(zb, c))

    def tiles(g, p, body):
        f0, fw = PASSES[p]

        @pl.loop(0, 4)
        def _(t2):
            @pl.loop(0, 4)
            def _(t1):
                for n0 in range(f0, f0 + fw, UNIT):
                    body((g, t2, t1, slice(None), pl.ds(n0, UNIT)))

    def combine(p, g):
        def body(at):
            sb[at] = (pb[at].astype(f32) + pr[at].astype(f32)).astype(bf16)

        tiles(g, p, body)
        for j in range(4):
            cs = pl.ds(*PASSES[p])
            put(
                None, sb.at[g, :, j, :, cs], sr.at[g, j, :, :, cs],
                k_ss.at[p, g, j], k_s.at[p, g, j], at_z(z, 1 - c),
            )

    def activate(p, g):
        for j in range(4):
            arrived(sr.at[g, j, :, :, pl.ds(*PASSES[p])], k_s.at[p, g, j])

        def grad(at):
            hid, back = sb[at].astype(f32), sr[at].astype(f32)
            square = hid * hid
            t = jnp.tanh(gelu_coef * (hid + cubic_coef * square * hid))
            slope = 0.5 * (1.0 + t) + 0.5 * hid * (1.0 - t * t) * gelu_coef * (1.0 + 3.0 * cubic_coef * square)
            gv[at] = (back * slope).astype(bf16)

        def act(at):
            hid = sr[at].astype(f32)
            t = jnp.tanh(gelu_coef * (hid + cubic_coef * hid * hid * hid))
            gv[at] = (0.5 * hid * (1.0 + t)).astype(bf16)

        @pl.when(c == 0)
        def _():
            tiles(g, p, grad)

        @pl.when(c == 1)
        def _():
            tiles(g, p, act)

    def grads_out(p, rel, part):
        zz, db, out = ((z, i, ga), (za, 1 - i, gb))[rel]
        r = pl.ds(part * 512, 512)
        for u in range(PASSES[p][0] // UNIT, sum(PASSES[p]) // UNIT):
            m, cc = u // 2, u % 2
            put(
                (c == cc) if rel == 0 else None,
                gs.at[db, r, pl.ds(u * UNIT, UNIT)], out.at[c, r, pl.ds(m * UNIT, UNIT)],
                k_gs.at[u, rel, part], k_g.at[m, rel, c, part], at_z(zz, cc),
            )

    def weight_grads(g):
        f0, fw = PASSES[0 if g is None else 1]
        cs = pl.ds(f0, fw)
        t, n = (slice(None), TOK) if g is None else (g, GROUP)
        for rel, db in ((1, 1 - i), (0, i)):
            for part in range(2):

                @pl.loop(0, 2)
                def _(j):
                    r = pl.ds(pl.multiple_of(part * 512 + j * 256, 256), 256)
                    total = mm(xv[db, t, :, :, :, r].reshape(n, 256), gv[t, :, :, :, cs].reshape(n, fw), 0, 0)
                    if g:
                        total = total + acc[db, r, :]
                    if g is None or g == 3:
                        gs[db, r, cs] = total.astype(bf16)
                    else:
                        acc[db, r, :] = total

                if g is None:
                    grads_out(0, rel, part)
                elif g == 3:
                    grads_out(1, rel, part)

    for k in range(3):
        for p2 in range(4):
            for p1 in range(4):
                at = (slice(None), p2, p1, slice(None), pl.ds(CHUNKS[k][0] * UNIT, CHUNKS[k][1] * UNIT))
                arrived(pr.at[at], k_b.at[k, p2 * 4 + p1])
    for g in range(4):
        combine(0, g)
        if g:
            activate(0, g - 1)
    activate(0, 3)
    weight_grads(None)

    def add_to(target, others):
        @pl.loop(0, 4)
        def _(t1):
            total = target[t1].astype(f32)
            for other in others:
                total = total + other[t1].astype(f32)
            target[t1] = total.astype(bf16)

    def line(g, o2, db):
        return ob.at[db, g, lax.rem(a2 + o2, 4)]

    def to_line(g, o2, db, side):
        put(
            None, line(g, o2, db), r1.at[g, side, db],
            k_r1s.at[g, side, db], k_r1.at[g, side, db], dev(0, o2),
        )

    def reduce_start(g):
        put(None, line(g, 2, 0), rl.at[g, 0], k_rls.at[g, 0], k_rl.at[g, 0], dev(0, 1))
        put(None, line(g, 2, 1), rl.at[g, 1], k_rls.at[g, 1], k_rl.at[g, 1], dev(0, 3))
        to_line(g, 1, 1, 0)
        to_line(g, 3, 0, 1)

    def reduce_relay(g):
        for db, o2 in ((0, 1), (1, 3)):
            arrived(rl.at[g, db], k_rl.at[g, db])
            add_to(line(g, o2, db), [rl.at[g, db]])
            to_line(g, o2, db, db)

    def reduce_line(g):
        for db in range(2):
            for side in range(2):
                arrived(r1.at[g, side, db], k_r1.at[g, side, db])
            add_to(line(g, 0, db), [r1.at[g, 0, db], r1.at[g, 1, db]])
        for o1 in (2, 1, 3):
            put(
                None, ob.at[:, g, a2, lax.rem(a1 + o1, 4)], r2.at[g, o1 - 1],
                k_r2s.at[g, o1 - 1], k_r2.at[g, o1 - 1], dev(o1, 0),
            )

    def finish(g):
        for o in range(3):
            arrived(r2.at[g, o], k_r2.at[g, o])
        for db in range(2):
            total = ob[db, g, a2, a1].astype(f32)
            for o in range(3):
                total = total + r2[g, o, db].astype(f32)
            fb[g, db] = total.astype(bf16)
        for rel, zz, db in ((1, za, 1 - i), (0, z, i)):
            put(
                (tau == c) if rel == 0 else None, fb.at[g, db], oo.at[c, g],
                k_os.at[g, rel], k_o.at[g, c], at_z(zz, tau),
            )

    for g in range(4):
        arrived(pr.at[late(g)], k_b2.at[g])
        combine(1, g)
        if g:
            weight_grads(g - 1)
            reduce_relay(g - 1)
        if g > 1:
            reduce_line(g - 2)
        activate(1, g)

        @pl.loop(0, 2)
        def _(db):
            @pl.loop(0, 2)
            def _(j):
                ds = pl.ds(pl.multiple_of(j * 512, 512), 512)
                prod = mm(gv[g].reshape(GROUP, HID), wv[db, ds, :], 1, 1)
                ob[db, g, :, :, :, ds] = prod.astype(bf16).reshape(4, 4, PIECE, 512)

        reduce_start(g)
    weight_grads(3)
    reduce_relay(3)
    finish(0)
    reduce_line(2)
    finish(1)
    reduce_line(3)
    finish(2)
    finish(3)

    for role in range(2):
        for g in range(4):
            arrived(oo.at[role, g], k_o.at[g, role])
        for m in range(4):
            for rel, out in ((0, ga), (1, gb)):
                for part in range(2):
                    arrived(
                        out.at[role, pl.ds(part * 512, 512), pl.ds(m * UNIT, UNIT)], k_g.at[m, rel, role, part]
                    )
    for local, copy in sends:
        if local is None:
            copy.wait_send()
        else:
            @pl.when(jnp.logical_not(local))
            def _():
                copy.wait_send()


def body(tokens, w_up, w_down, cotangent):
    batch_total = tokens.shape[0] * lax.axis_size("col") * lax.axis_size("dp")
    grad_scale = float(batch_total) ** (-0.5)
    dma = pltpu.SemaphoreType.DMA
    anywhere = pl.BlockSpec(memory_space=pl.ANY)
    oo, ga, gb = pl.pallas_call(
        kernel,
        out_shape=(
            jax.ShapeDtypeStruct((2, 4, PIECE, WIDE), bf16),
            jax.ShapeDtypeStruct((2, WIDE, SLICE), bf16),
            jax.ShapeDtypeStruct((2, WIDE, SLICE), bf16),
        ),
        in_specs=[anywhere] * 4,
        out_specs=(anywhere,) * 3,
        scratch_shapes=[
            pltpu.VMEM((2, 4, 4, 4, PIECE, WIDE), bf16),
            pltpu.VMEM((2, WIDE, HID), bf16),
            pltpu.VMEM((4, 4, 4, PIECE, HID), bf16),
            pltpu.VMEM((4, 4, 4, PIECE, HID), bf16),
            pltpu.VMEM((4, 4, 4, PIECE, HID), bf16),
            pltpu.VMEM((4, 4, 4, PIECE, HID), bf16),
            pltpu.VMEM((4, 4, 4, PIECE, HID), bf16),
            pltpu.VMEM((2, 4, 4, 4, PIECE, WIDE), bf16),
            pltpu.VMEM((4, 2, 2, 4, PIECE, WIDE), bf16),
            pltpu.VMEM((4, 2, 4, PIECE, WIDE), bf16),
            pltpu.VMEM((4, 3, 2, PIECE, WIDE), bf16),
            pltpu.VMEM((4, 2, PIECE, WIDE), bf16),
            pltpu.VMEM((2, WIDE, HID), bf16),
            pltpu.VMEM((2, WIDE, PASSES[1][1]), f32),
            dma((2,)), dma((2, 16)),
            dma((4, 2, 2)), dma((8, 2)),
            dma((30,)),
            dma((3, 16)), dma((3, 16)), dma((4,)), dma((4,)),
            dma((2, 4, 4)), dma((2, 4, 4)),
            dma((4, 2, 2)), dma((4, 2, 2)), dma((4, 2)), dma((4, 2)),
            dma((4, 3)), dma((4, 3)),
            dma((8, 2, 2)), dma((4, 2, 2, 2)),
            dma((4, 2)), dma((4, 2)),
        ],
        compiler_params=pltpu.CompilerParams(
            collective_id=0, has_side_effects=True, vmem_limit_bytes=63 << 20
        ),
        name="ffn",
    )(tokens.reshape(4, PIECE, WIDE), cotangent.reshape(4, PIECE, WIDE), w_up, w_down)
    oo = oo.reshape(2, SHARD, WIDE)
    up_grad = grad_scale * (ga[0].astype(f32) + gb[0].astype(f32))
    down_grad = grad_scale * (ga[1].astype(f32) + gb[1].astype(f32))
    return (oo[1], oo[0], up_grad, down_grad)


def solution(mesh):
    placed = (P(("dp", "col"), "row"), P("row", "col"), P("row", "col"), P(("dp", "col"), "row"))
    return jax.shard_map(
        body,
        mesh=mesh,
        in_specs=placed,
        out_specs=(
            P(("dp", "col"), "row"),
            P(("dp", "col"), "row"),
            P("row", ("col", "dp")),
            P("row", ("col", "dp")),
        ),
        check_vma=False,
    )
```

```python
import jax
import jax.numpy as jnp
from jax import lax
from jax.experimental import pallas as pl
from jax.experimental.pallas import tpu as pltpu
from jax.sharding import PartitionSpec as P

MESH = pl.DeviceIdType.MESH
bf16 = jnp.bfloat16
f32 = jnp.float32
gelu_coef = 0.7978845608
cubic_coef = 0.044715

SHARD = 128
WIDE = 1024
SLICE = 512
TOK = 16 * SHARD
HID = 2 * SLICE
UNIT = 128
CHUNKS = ((0, 2), (2, 1), (3, 1), (4, 4))
EARLY = 4 * UNIT
PASSES = ((0, EARLY), (EARLY, HID - EARLY))
PIECE = SHARD // 4
GROUP = 16 * PIECE


def mm(left, right, dim_left, dim_right):
    return lax.dot_general(
        left, right, (((dim_left,), (dim_right,)), ((), ())), preferred_element_type=f32
    )


def kernel(
    tok, cot, wup, wdn, oo, ga, gb,
    xv, wv, pb, pr, sb, sr, gv, ob, r1, rl, r2, fb, gs, acc,
    k_xin, k_x, k_ws, k_w, k_ag, k_bs, k_b, k_bs2, k_b2, k_ss, k_s, k_ts, k_t,
    k_r1s, k_r1, k_rls, k_rl, k_r2s, k_r2, k_gs, k_g, k_os, k_o,
):
    dp, z, c = lax.axis_index("dp"), lax.axis_index("row"), lax.axis_index("col")
    y, x = lax.div(dp, 4), lax.rem(dp, 4)
    half, i = lax.div(z, 2), lax.rem(z, 2)
    za, zb = z + 1 - 2 * i, 3 - z
    tau = lax.rem(lax.div(z + 1, 2), 2)

    def remote(src, dst, send, recv, dev):
        return pltpu.make_async_remote_copy(
            src_ref=src, dst_ref=dst, send_sem=send, recv_sem=recv, device_id=dev, device_id_type=MESH
        )

    def arrived(dst, sem):
        pltpu.make_async_copy(dst, dst, sem).wait()

    a1, a2 = x * (1 - c) + y * c, y * (1 - c) + x * c

    def place(o1, o2):
        return lax.rem(a2 + o2, 4), lax.rem(a1 + o1, 4)

    def number(p):
        return p[0] * 4 + p[1]

    def dev(o1, o2):
        p2, p1 = place(o1, o2)
        return {"dp": (p1 * c + p2 * (1 - c)) * 4 + p1 * (1 - c) + p2 * c, "row": z, "col": c}

    def at_z(zz, cc):
        return {"dp": dp, "row": zz, "col": cc}

    sends = []

    def put(local, src, dst, send, recv, to):
        copy = remote(src, dst, send, recv, to)
        if local is None:
            copy.start()
        else:
            @pl.when(local)
            def _():
                pltpu.make_async_copy(src, dst, recv).start()

            @pl.when(jnp.logical_not(local))
            def _():
                copy.start()
        sends.append((local, copy))

    barrier = pltpu.get_barrier_semaphore()
    peers = [at_z(za, 0), at_z(za, 1), at_z(zb, c), at_z(z, 1 - c)]
    peers += [dev(o, 0) for o in (1, 2, 3)] + [dev(0, o) for o in (1, 2, 3)]
    for peer in peers:
        pl.semaphore_signal(barrier, inc=1, device_id=peer, device_id_type=MESH)
    pl.semaphore_wait(barrier, len(peers))

    own = place(0, 0)
    here = c == tau
    zx = z * (1 - lax.rem(c + tau, 2)) + za * lax.rem(c + tau, 2)
    for role, src, p in ((0, tok, (y, x)), (1, cot, (x, y))):
        put(
            jnp.logical_and(here, c == role), src, xv.at[i, :, p[0], p[1]],
            k_xin.at[role], k_x.at[i, number(p)], at_z(zx, role),
        )
    for m in range(4):
        u = 2 * m + c
        cols = pl.ds(pl.multiple_of(dp * SLICE + m * UNIT, UNIT), UNIT)
        into = pl.ds(pl.multiple_of(u * UNIT, UNIT), UNIT)
        for rel, zz in ((1, za), (0, z)):
            for role, src in ((0, wup), (1, wdn)):
                put(
                    (c == role) if rel == 0 else None, src.at[:, cols], wv.at[i, :, into],
                    k_ws.at[m, rel, role], k_w.at[u, i], at_z(zz, role),
                )

    def weights(k):
        u0, n = CHUNKS[k]
        for u in range(u0, u0 + n):
            for db in range(2):
                arrived(wv.at[db, :, pl.ds(u * UNIT, UNIT)], k_w.at[u, db])

    count = [0]

    def shard_to(db, p, to):
        part = xv.at[db, :, p[0], p[1]]
        put(None, part, part, k_ag.at[count[0]], k_x.at[db, number(p)], to)
        count[0] += 1

    def shard_in(db, p):
        arrived(xv.at[db, :, p[0], p[1]], k_x.at[db, number(p)])

    def hidden(part, m, shape, f0, fw):
        cs = pl.ds(f0, fw)
        total = [mm(xv[(db, *part)].reshape(m, WIDE), wv[db, :, cs], 1, 0) for db in range(2)]
        pb[(*part, slice(None), cs)] = (total[0] + total[1]).astype(bf16).reshape(*shape, PIECE, fw)

    expected = {}

    def hidden_set(shards, first, last):
        n, offsets = shards
        u0, u1 = CHUNKS[first][0], sum(CHUNKS[last])
        f0, fw = u0 * UNIT, (u1 - u0) * UNIT

        @pl.loop(0, n)
        def _(j):
            p = place(*offsets(j))
            hidden((slice(None), p[0], p[1]), SHARD, (4,), f0, fw)

        for j in range(n):
            o = offsets(j)
            p = place(*o)
            at = (slice(None), p[0], p[1], slice(None), pl.ds(f0, fw))
            sem = k_b.at[first, number(p)]
            put(None, pb.at[at], pr.at[at], k_bs.at[first, number(p)], sem, at_z(zb, c))
            expected.setdefault(o, []).append((at, sem))

    halves = (i, 1 - i)

    def across(o1, o2):
        p = place(o1, o2)
        for way, db in enumerate(halves):
            shard_in(db, p)
            if (o2, way) in ((3, 0), (1, 1)):
                shard_to(db, p, dev(0, 4 - o2))

    centre, beside = (3, lambda j: (0, (j + 3) % 4)), (3, lambda j: (j + 1, 0))
    low, high, across_far = (2, lambda j: (3, 3 - 2 * j)), (2, lambda j: (1, 3 - 2 * j)), (1, lambda j: (0, 2))
    edge = (2, lambda j: (2, 3 - 2 * j))
    corners = [(1, lambda j, o1=o1: (o1, 2)) for o1 in (3, 1, 2)]
    for db in halves:
        shard_in(db, own)
        for to in (dev(1, 0), dev(3, 0), dev(0, 1), dev(0, 3)):
            shard_to(db, own, to)
    for o1 in (3, 1):
        p = place(o1, 0)
        for way, db in enumerate(halves):
            shard_in(db, p)
            if (o1, way) in ((3, 0), (1, 1)):
                shard_to(db, p, dev(4 - o1, 0))
            for to in (dev(0, 1), dev(0, 3)):
                shard_to(db, p, to)
    across(0, 3)
    across(0, 1)
    for db in halves:
        shard_in(db, place(2, 0))
        for to in (dev(0, 1), dev(0, 3)):
            shard_to(db, place(2, 0), to)
    weights(0)
    hidden_set(centre, 0, 0)
    hidden_set(beside, 0, 0)
    across(3, 3)
    across(3, 1)
    hidden_set(low, 0, 0)
    weights(1)
    for shards in (centre, beside, low):
        hidden_set(shards, 1, 1)
    across(1, 3)
    across(1, 1)
    hidden_set(high, 0, 1)
    across(0, 2)
    hidden_set(across_far, 0, 1)
    weights(2)
    for shards in (centre, beside, low, high, across_far):
        hidden_set(shards, 2, 2)
    across(2, 3)
    across(2, 1)
    hidden_set(edge, 0, 2)
    for shards in corners:
        across(*shards[1](0))
        hidden_set(shards, 0, 2)
    weights(3)
    f2, w2 = PASSES[1]

    def late(g):
        return (g, slice(None), slice(None), slice(None), pl.ds(f2, w2))

    for g in range(4):
        hidden((g, slice(None), slice(None)), GROUP, (4, 4), f2, w2)
        put(None, pb.at[late(g)], pr.at[late(g)], k_bs2.at[g], k_b2.at[g], at_z(zb, c))

    def columns(p, body):
        f0, fw = PASSES[p]
        for n0 in range(f0, f0 + fw, UNIT):
            body(pl.ds(n0, UNIT))

    def over_set(shards, body):
        @pl.loop(0, shards[0])
        def _(j):
            p2, p1 = place(*shards[1](j))

            @pl.loop(0, 4)
            def _(g):
                columns(0, lambda cs: body((g, p2, p1, slice(None), cs)))

    def over_group(g, body):
        @pl.loop(0, 4)
        def _(p2):
            @pl.loop(0, 4)
            def _(p1):
                columns(1, lambda cs: body((g, p2, p1, slice(None), cs)))

    def add_pair(at):
        sb[at] = (pb[at].astype(f32) + pr[at].astype(f32)).astype(bf16)

    def grad(at):
        hid, back = sb[at].astype(f32), sr[at].astype(f32)
        square = hid * hid
        t = jnp.tanh(gelu_coef * (hid + cubic_coef * square * hid))
        slope = 0.5 * (1.0 + t) + 0.5 * hid * (1.0 - t * t) * gelu_coef * (1.0 + 3.0 * cubic_coef * square)
        gv[at] = (back * slope).astype(bf16)

    def act(at):
        hid = sr[at].astype(f32)
        t = jnp.tanh(gelu_coef * (hid + cubic_coef * hid * hid * hid))
        gv[at] = (0.5 * hid * (1.0 + t)).astype(bf16)

    def combine_set(shards):
        cs = pl.ds(*PASSES[0])
        places = [shards[1](j) for j in range(shards[0])]
        for o in places:
            for at, sem in expected[o]:
                arrived(pr.at[at], sem)
        over_set(shards, add_pair)
        for o in places:
            p2, p1 = place(*o)
            put(
                None, sb.at[:, p2, p1, :, cs], sr.at[:, p1, p2, :, cs],
                k_ss.at[p2 * 4 + p1], k_s.at[p1 * 4 + p2], at_z(z, 1 - c),
            )

    def activate_sets(sets):
        for shards in sets:
            for j in range(shards[0]):
                p2, p1 = place(*shards[1](j))
                arrived(sr.at[:, p2, p1, :, pl.ds(*PASSES[0])], k_s.at[p2 * 4 + p1])
        for role, body in ((0, grad), (1, act)):

            @pl.when(c == role)
            def _():
                for shards in sets:
                    over_set(shards, body)

    def combine(g):
        over_group(g, add_pair)
        for j in range(4):
            cs = pl.ds(*PASSES[1])
            put(
                None, sb.at[g, :, j, :, cs], sr.at[g, j, :, :, cs],
                k_ts.at[g, j], k_t.at[g, j], at_z(z, 1 - c),
            )

    def activate(g):
        for j in range(4):
            arrived(sr.at[g, j, :, :, pl.ds(*PASSES[1])], k_t.at[g, j])
        for role, body in ((0, grad), (1, act)):

            @pl.when(c == role)
            def _():
                over_group(g, body)

    def grads_out(p, rel, part):
        zz, db, out = ((z, i, ga), (za, 1 - i, gb))[rel]
        r = pl.ds(part * 512, 512)
        for u in range(PASSES[p][0] // UNIT, sum(PASSES[p]) // UNIT):
            m, cc = u // 2, u % 2
            put(
                (c == cc) if rel == 0 else None,
                gs.at[db, r, pl.ds(u * UNIT, UNIT)], out.at[c, r, pl.ds(m * UNIT, UNIT)],
                k_gs.at[u, rel, part], k_g.at[m, rel, c, part], at_z(zz, cc),
            )

    def weight_grads(g, rels=(1, 0)):
        f0, fw = PASSES[0 if g is None else 1]
        cs = pl.ds(f0, fw)
        t, n = (slice(None), TOK) if g is None else (g, GROUP)
        for rel in rels:
            db = (i, 1 - i)[rel]
            for part in range(2):

                @pl.loop(0, 2)
                def _(j):
                    r = pl.ds(pl.multiple_of(part * 512 + j * 256, 256), 256)
                    total = mm(xv[db, t, :, :, :, r].reshape(n, 256), gv[t, :, :, :, cs].reshape(n, fw), 0, 0)
                    if g:
                        total = total + acc[db, r, :]
                    if g is None or g == 3:
                        gs[db, r, cs] = total.astype(bf16)
                    else:
                        acc[db, r, :] = total

                if g is None:
                    grads_out(0, rel, part)
                elif g == 3:
                    grads_out(1, rel, part)

    for shards in (centre, beside, low, high, across_far):
        combine_set(shards)
    block = (9, lambda j: ((j % 3 + 3) % 4, (j // 3 + 3) % 4))
    activate_sets([block, (2, lambda j: (2 * j, 2 - 2 * j))])
    for shards in (edge, *corners):
        combine_set(shards)
    activate_sets([edge, (3, lambda j: ((j + 1) % 4, 2))])

    def add_to(target, others):
        @pl.loop(0, 4)
        def _(t1):
            total = target[t1].astype(f32)
            for other in others:
                total = total + other[t1].astype(f32)
            target[t1] = total.astype(bf16)

    def line(g, o2, db):
        return ob.at[db, g, lax.rem(a2 + o2, 4)]

    def to_line(g, o2, db, side):
        put(
            None, line(g, o2, db), r1.at[g, side, db],
            k_r1s.at[g, side, db], k_r1.at[g, side, db], dev(0, o2),
        )

    def reduce_start(g):
        put(None, line(g, 2, 0), rl.at[g, 0], k_rls.at[g, 0], k_rl.at[g, 0], dev(0, 1))
        put(None, line(g, 2, 1), rl.at[g, 1], k_rls.at[g, 1], k_rl.at[g, 1], dev(0, 3))
        to_line(g, 1, 1, 0)
        to_line(g, 3, 0, 1)

    def reduce_relay(g):
        for db, o2 in ((0, 1), (1, 3)):
            arrived(rl.at[g, db], k_rl.at[g, db])
            add_to(line(g, o2, db), [rl.at[g, db]])
            to_line(g, o2, db, db)

    def reduce_line(g):
        for db in range(2):
            for side in range(2):
                arrived(r1.at[g, side, db], k_r1.at[g, side, db])
            add_to(line(g, 0, db), [r1.at[g, 0, db], r1.at[g, 1, db]])
        for o1 in (2, 1, 3):
            put(
                None, ob.at[:, g, a2, lax.rem(a1 + o1, 4)], r2.at[g, o1 - 1],
                k_r2s.at[g, o1 - 1], k_r2.at[g, o1 - 1], dev(o1, 0),
            )

    def finish(g):
        for o in range(3):
            arrived(r2.at[g, o], k_r2.at[g, o])
        for db in range(2):
            total = ob[db, g, a2, a1].astype(f32)
            for o in range(3):
                total = total + r2[g, o, db].astype(f32)
            fb[g, db] = total.astype(bf16)
        for rel, zz, db in ((1, za, 1 - i), (0, z, i)):
            put(
                (tau == c) if rel == 0 else None, fb.at[g, db], oo.at[c, g],
                k_os.at[g, rel], k_o.at[g, c], at_z(zz, tau),
            )

    def out(g):
        @pl.loop(0, 2)
        def _(db):
            @pl.loop(0, 2)
            def _(j):
                ds = pl.ds(pl.multiple_of(j * 512, 512), 512)
                prod = mm(gv[g].reshape(GROUP, HID), wv[db, ds, :], 1, 1)
                ob[db, g, :, :, :, ds] = prod.astype(bf16).reshape(4, 4, PIECE, 512)

    for g in range(4):
        if g == 0:
            weight_grads(None, (1,))
        arrived(pr.at[late(g)], k_b2.at[g])
        combine(g)
        if g == 0:
            weight_grads(None, (0,))
        else:
            weight_grads(g - 1)
            reduce_relay(g - 1)
        if g > 1:
            reduce_line(g - 2)
        activate(g)
        if g == 3:
            weight_grads(3, (1,))
        out(g)
        reduce_start(g)
    weight_grads(3, (0,))
    reduce_relay(3)
    finish(0)
    reduce_line(2)
    finish(1)
    reduce_line(3)
    finish(2)
    finish(3)

    for role in range(2):
        for g in range(4):
            arrived(oo.at[role, g], k_o.at[g, role])
        for m in range(4):
            for rel, out in ((0, ga), (1, gb)):
                for part in range(2):
                    arrived(
                        out.at[role, pl.ds(part * 512, 512), pl.ds(m * UNIT, UNIT)], k_g.at[m, rel, role, part]
                    )
    for local, copy in sends:
        if local is None:
            copy.wait_send()
        else:
            @pl.when(jnp.logical_not(local))
            def _():
                copy.wait_send()


def body(tokens, w_up, w_down, cotangent):
    batch_total = tokens.shape[0] * lax.axis_size("col") * lax.axis_size("dp")
    grad_scale = float(batch_total) ** (-0.5)
    dma = pltpu.SemaphoreType.DMA
    anywhere = pl.BlockSpec(memory_space=pl.ANY)
    oo, ga, gb = pl.pallas_call(
        kernel,
        out_shape=(
            jax.ShapeDtypeStruct((2, 4, PIECE, WIDE), bf16),
            jax.ShapeDtypeStruct((2, WIDE, SLICE), bf16),
            jax.ShapeDtypeStruct((2, WIDE, SLICE), bf16),
        ),
        in_specs=[anywhere] * 4,
        out_specs=(anywhere,) * 3,
        scratch_shapes=[
            pltpu.VMEM((2, 4, 4, 4, PIECE, WIDE), bf16),
            pltpu.VMEM((2, WIDE, HID), bf16),
            pltpu.VMEM((4, 4, 4, PIECE, HID), bf16),
            pltpu.VMEM((4, 4, 4, PIECE, HID), bf16),
            pltpu.VMEM((4, 4, 4, PIECE, HID), bf16),
            pltpu.VMEM((4, 4, 4, PIECE, HID), bf16),
            pltpu.VMEM((4, 4, 4, PIECE, HID), bf16),
            pltpu.VMEM((2, 4, 4, 4, PIECE, WIDE), bf16),
            pltpu.VMEM((4, 2, 2, 4, PIECE, WIDE), bf16),
            pltpu.VMEM((4, 2, 4, PIECE, WIDE), bf16),
            pltpu.VMEM((4, 3, 2, PIECE, WIDE), bf16),
            pltpu.VMEM((4, 2, PIECE, WIDE), bf16),
            pltpu.VMEM((2, WIDE, HID), bf16),
            pltpu.VMEM((2, WIDE, PASSES[1][1]), f32),
            dma((2,)), dma((2, 16)),
            dma((4, 2, 2)), dma((8, 2)),
            dma((30,)),
            dma((3, 16)), dma((3, 16)), dma((4,)), dma((4,)),
            dma((16,)), dma((16,)), dma((4, 4)), dma((4, 4)),
            dma((4, 2, 2)), dma((4, 2, 2)), dma((4, 2)), dma((4, 2)),
            dma((4, 3)), dma((4, 3)),
            dma((8, 2, 2)), dma((4, 2, 2, 2)),
            dma((4, 2)), dma((4, 2)),
        ],
        compiler_params=pltpu.CompilerParams(
            collective_id=0, has_side_effects=True, vmem_limit_bytes=63 << 20
        ),
        name="ffn",
    )(tokens.reshape(4, PIECE, WIDE), cotangent.reshape(4, PIECE, WIDE), w_up, w_down)
    oo = oo.reshape(2, SHARD, WIDE)
    up_grad = grad_scale * (ga[0].astype(f32) + gb[0].astype(f32))
    down_grad = grad_scale * (ga[1].astype(f32) + gb[1].astype(f32))
    return (oo[1], oo[0], up_grad, down_grad)


def solution(mesh):
    placed = (P(("dp", "col"), "row"), P("row", "col"), P("row", "col"), P(("dp", "col"), "row"))
    return jax.shard_map(
        body,
        mesh=mesh,
        in_specs=placed,
        out_specs=(
            P(("dp", "col"), "row"),
            P(("dp", "col"), "row"),
            P("row", ("col", "dp")),
            P("row", ("col", "dp")),
        ),
        check_vma=False,
    )
```

```python
import functools

import jax
import jax.numpy as jnp
from jax import lax
from jax.experimental import pallas as pl
from jax.experimental.pallas import tpu as pltpu
from jax.sharding import PartitionSpec as P

MESH = pl.DeviceIdType.MESH
bf16 = jnp.bfloat16
f32 = jnp.float32
gelu_coef = 0.7978845608
cubic_coef = 0.044715

SHARD = 128
WIDE = 1024
SLICE = 512
TOK = 16 * SHARD
HID = 2 * SLICE
UNIT = 128
CHUNKS = ((0, 2), (2, 2), (4, 4))
EARLY = 4 * UNIT
PASSES = ((0, EARLY), (EARLY, HID - EARLY))
PIECE = SHARD // 4
GROUP = 16 * PIECE


def mm(left, right, dim_left, dim_right):
    return lax.dot_general(
        left, right, (((dim_left,), (dim_right,)), ((), ())), preferred_element_type=f32
    )


def kernel(
    tok, cot, wup, wdn, oo, ga, gb,
    xv, wv, pb, pr, sb, sr, gv, ob, r1, rl, r2, fb, gs, acc,
    k_xin, k_x, k_ws, k_w, k_ag, k_bs, k_b, k_bs2, k_b2, k_ss, k_s, k_ts, k_t,
    k_r1s, k_r1, k_rls, k_rl, k_r2s, k_r2, k_gs, k_g, k_os, k_o,
):
    dp, z, c = lax.axis_index("dp"), lax.axis_index("row"), lax.axis_index("col")
    y, x = lax.div(dp, 4), lax.rem(dp, 4)
    half, i = lax.div(z, 2), lax.rem(z, 2)
    za, zb = z + 1 - 2 * i, 3 - z
    tau = lax.rem(lax.div(z + 1, 2), 2)

    def remote(src, dst, send, recv, dev):
        return pltpu.make_async_remote_copy(
            src_ref=src, dst_ref=dst, send_sem=send, recv_sem=recv, device_id=dev, device_id_type=MESH
        )

    def arrived(dst, sem):
        pltpu.make_async_copy(dst, dst, sem).wait()

    a1, a2 = x * (1 - c) + y * c, y * (1 - c) + x * c

    def place(o1, o2):
        return lax.rem(a2 + o2, 4), lax.rem(a1 + o1, 4)

    def number(p):
        return p[0] * 4 + p[1]

    def dev(o1, o2):
        p2, p1 = place(o1, o2)
        return {"dp": (p1 * c + p2 * (1 - c)) * 4 + p1 * (1 - c) + p2 * c, "row": z, "col": c}

    def at_z(zz, cc):
        return {"dp": dp, "row": zz, "col": cc}

    sends = []

    def put(local, src, dst, send, recv, to):
        copy = remote(src, dst, send, recv, to)
        if local is None:
            copy.start()
        else:
            @pl.when(local)
            def _():
                pltpu.make_async_copy(src, dst, recv).start()

            @pl.when(jnp.logical_not(local))
            def _():
                copy.start()
        sends.append((local, copy))

    barrier = pltpu.get_barrier_semaphore()
    peers = [at_z(za, 0), at_z(za, 1), at_z(zb, c), at_z(z, 1 - c)]
    peers += [dev(o, 0) for o in (1, 2, 3)] + [dev(0, o) for o in (1, 2, 3)]
    for peer in peers:
        pl.semaphore_signal(barrier, inc=1, device_id=peer, device_id_type=MESH)
    pl.semaphore_wait(barrier, len(peers))

    own = place(0, 0)
    here = c == tau
    zx = z * (1 - lax.rem(c + tau, 2)) + za * lax.rem(c + tau, 2)
    for role, src, p in ((0, tok, (y, x)), (1, cot, (x, y))):
        put(
            jnp.logical_and(here, c == role), src, xv.at[i, :, p[0], p[1]],
            k_xin.at[role], k_x.at[i, number(p)], at_z(zx, role),
        )
    for m in range(4):
        u = 2 * m + c
        cols = pl.ds(pl.multiple_of(dp * SLICE + m * UNIT, UNIT), UNIT)
        into = pl.ds(pl.multiple_of(u * UNIT, UNIT), UNIT)
        for rel, zz in ((1, za), (0, z)):
            for role, src in ((0, wup), (1, wdn)):
                put(
                    (c == role) if rel == 0 else None, src.at[:, cols], wv.at[i, :, into],
                    k_ws.at[m, rel, role], k_w.at[u, i], at_z(zz, role),
                )

    def weights(k):
        u0, n = CHUNKS[k]
        for u in range(u0, u0 + n):
            for db in range(2):
                arrived(wv.at[db, :, pl.ds(u * UNIT, UNIT)], k_w.at[u, db])

    count = [0]

    def shard_to(db, p, to):
        part = xv.at[db, :, p[0], p[1]]
        put(None, part, part, k_ag.at[count[0]], k_x.at[db, number(p)], to)
        count[0] += 1

    def shard_in(db, p):
        arrived(xv.at[db, :, p[0], p[1]], k_x.at[db, number(p)])

    def hidden(part, m, shape, f0, fw):
        cs = pl.ds(f0, fw)
        total = [mm(xv[(db, *part)].reshape(m, WIDE), wv[db, :, cs], 1, 0) for db in range(2)]
        pb[(*part, slice(None), cs)] = (total[0] + total[1]).astype(bf16).reshape(*shape, PIECE, fw)

    expected = {}

    def hidden_set(shards, first, last):
        n, offsets = shards
        u0, u1 = CHUNKS[first][0], sum(CHUNKS[last])
        f0, fw = u0 * UNIT, (u1 - u0) * UNIT

        @pl.loop(0, n)
        def _(j):
            p = place(*offsets(j))
            hidden((slice(None), p[0], p[1]), SHARD, (4,), f0, fw)

        for j in range(n):
            o = offsets(j)
            p = place(*o)
            at = (slice(None), p[0], p[1], slice(None), pl.ds(f0, fw))
            sem = k_b.at[first, number(p)]
            put(None, pb.at[at], pr.at[at], k_bs.at[first, number(p)], sem, at_z(zb, c))
            expected.setdefault(o, []).append((at, sem))

    halves = (i, 1 - i)

    def across(o1, o2):
        p = place(o1, o2)
        for way, db in enumerate(halves):
            shard_in(db, p)
            if (o2, way) in ((3, 0), (1, 1)):
                shard_to(db, p, dev(0, 4 - o2))

    centre, beside = (3, lambda j: (0, (j + 3) % 4)), (3, lambda j: (j + 1, 0))
    low, high, across_far = (2, lambda j: (3, 3 - 2 * j)), (2, lambda j: (1, 3 - 2 * j)), (1, lambda j: (0, 2))
    edge = (2, lambda j: (2, 3 - 2 * j))
    corners = [(1, lambda j, o1=o1: (o1, 2)) for o1 in (3, 1, 2)]
    for db in halves:
        shard_in(db, own)
        for to in (dev(1, 0), dev(3, 0), dev(0, 1), dev(0, 3)):
            shard_to(db, own, to)
    for o1 in (3, 1):
        p = place(o1, 0)
        for way, db in enumerate(halves):
            shard_in(db, p)
            if (o1, way) in ((3, 0), (1, 1)):
                shard_to(db, p, dev(4 - o1, 0))
            for to in (dev(0, 1), dev(0, 3)):
                shard_to(db, p, to)
    across(0, 3)
    across(0, 1)
    for db in halves:
        shard_in(db, place(2, 0))
        for to in (dev(0, 1), dev(0, 3)):
            shard_to(db, place(2, 0), to)
    weights(0)
    hidden_set(centre, 0, 0)
    hidden_set(beside, 0, 0)
    across(3, 3)
    across(3, 1)
    hidden_set(low, 0, 0)
    weights(1)
    for shards in (centre, beside, low):
        hidden_set(shards, 1, 1)
    across(1, 3)
    across(1, 1)
    hidden_set(high, 0, 1)
    across(0, 2)
    hidden_set(across_far, 0, 1)
    across(2, 3)
    across(2, 1)
    hidden_set(edge, 0, 1)
    for shards in corners:
        across(*shards[1](0))
        hidden_set(shards, 0, 1)
    weights(2)
    f2, w2 = PASSES[1]

    def late(g):
        return (g, slice(None), slice(None), slice(None), pl.ds(f2, w2))

    for g in range(4):
        hidden((g, slice(None), slice(None)), GROUP, (4, 4), f2, w2)
        put(None, pb.at[late(g)], pr.at[late(g)], k_bs2.at[g], k_b2.at[g], at_z(zb, c))

    def columns(p, body):
        f0, fw = PASSES[p]
        for n0 in range(f0, f0 + fw, UNIT):
            body(pl.ds(n0, UNIT))

    def over_set(shards, body):
        @pl.loop(0, shards[0])
        def _(j):
            p2, p1 = place(*shards[1](j))

            @pl.loop(0, 4)
            def _(g):
                columns(0, lambda cs: body((g, p2, p1, slice(None), cs)))

    def over_group(g, body):
        @pl.loop(0, 4)
        def _(p2):
            @pl.loop(0, 4)
            def _(p1):
                columns(1, lambda cs: body((g, p2, p1, slice(None), cs)))

    def add_pair(at):
        sb[at] = (pb[at].astype(f32) + pr[at].astype(f32)).astype(bf16)

    def grad(at):
        hid, back = sb[at].astype(f32), sr[at].astype(f32)
        square = hid * hid
        t = jnp.tanh(gelu_coef * (hid + cubic_coef * square * hid))
        slope = 0.5 * (1.0 + t) + 0.5 * hid * (1.0 - t * t) * gelu_coef * (1.0 + 3.0 * cubic_coef * square)
        gv[at] = (back * slope).astype(bf16)

    def act(at):
        hid = sr[at].astype(f32)
        t = jnp.tanh(gelu_coef * (hid + cubic_coef * hid * hid * hid))
        gv[at] = (0.5 * hid * (1.0 + t)).astype(bf16)

    def combine_set(shards):
        cs = pl.ds(*PASSES[0])
        places = [shards[1](j) for j in range(shards[0])]
        for o in places:
            for at, sem in expected[o]:
                arrived(pr.at[at], sem)
        over_set(shards, add_pair)
        for o in places:
            p2, p1 = place(*o)
            put(
                None, sb.at[:, p2, p1, :, cs], sr.at[:, p1, p2, :, cs],
                k_ss.at[p2 * 4 + p1], k_s.at[p1 * 4 + p2], at_z(z, 1 - c),
            )

    def activate_sets(sets):
        for shards in sets:
            for j in range(shards[0]):
                p2, p1 = place(*shards[1](j))
                arrived(sr.at[:, p2, p1, :, pl.ds(*PASSES[0])], k_s.at[p2 * 4 + p1])
        for role, body in ((0, grad), (1, act)):

            @pl.when(c == role)
            def _():
                for shards in sets:
                    over_set(shards, body)

    def combine(g):
        over_group(g, add_pair)
        for j in range(4):
            cs = pl.ds(*PASSES[1])
            put(
                None, sb.at[g, :, j, :, cs], sr.at[g, j, :, :, cs],
                k_ts.at[g, j], k_t.at[g, j], at_z(z, 1 - c),
            )

    def activate(g):
        for j in range(4):
            arrived(sr.at[g, j, :, :, pl.ds(*PASSES[1])], k_t.at[g, j])
        for role, body in ((0, grad), (1, act)):

            @pl.when(c == role)
            def _():
                over_group(g, body)

    def grads_out(p, rel, part):
        zz, db, out = ((z, i, ga), (za, 1 - i, gb))[rel]
        r = pl.ds(part * 512, 512)
        for u in range(PASSES[p][0] // UNIT, sum(PASSES[p]) // UNIT):
            m, cc = u // 2, u % 2
            put(
                (c == cc) if rel == 0 else None,
                gs.at[db, r, pl.ds(u * UNIT, UNIT)], out.at[c, r, pl.ds(m * UNIT, UNIT)],
                k_gs.at[u, rel, part], k_g.at[m, rel, c, part], at_z(zz, cc),
            )

    def weight_grads(g, rels=(1, 0)):
        f0, fw = PASSES[0 if g is None else 1]
        cs = pl.ds(f0, fw)
        t, n = (slice(None), TOK) if g is None else (g, GROUP)
        for rel in rels:
            db = (i, 1 - i)[rel]
            for part in range(2):

                @pl.loop(0, 2)
                def _(j):
                    r = pl.ds(pl.multiple_of(part * 512 + j * 256, 256), 256)
                    total = mm(xv[db, t, :, :, :, r].reshape(n, 256), gv[t, :, :, :, cs].reshape(n, fw), 0, 0)
                    if g:
                        total = total + acc[db, r, :]
                    if g is None or g == 3:
                        gs[db, r, cs] = total.astype(bf16)
                    else:
                        acc[db, r, :] = total

                if g is None:
                    grads_out(0, rel, part)
                elif g == 3:
                    grads_out(1, rel, part)

    for shards in (centre, beside, low, high, across_far):
        combine_set(shards)
    block = (9, lambda j: ((j % 3 + 3) % 4, (j // 3 + 3) % 4))
    activate_sets([block, (2, lambda j: (2 * j, 2 - 2 * j))])
    for shards in (edge, *corners):
        combine_set(shards)
    activate_sets([edge, (3, lambda j: ((j + 1) % 4, 2))])

    def add_to(target, others):
        @pl.loop(0, 4)
        def _(t1):
            total = target[t1].astype(f32)
            for other in others:
                total = total + other[t1].astype(f32)
            target[t1] = total.astype(bf16)

    def line(g, o2, db):
        return ob.at[db, g, lax.rem(a2 + o2, 4)]

    def to_line(g, o2, db, side):
        put(
            None, line(g, o2, db), r1.at[g, side, db],
            k_r1s.at[g, side, db], k_r1.at[g, side, db], dev(0, o2),
        )

    def reduce_start(g):
        put(None, line(g, 2, 0), rl.at[g, 0], k_rls.at[g, 0], k_rl.at[g, 0], dev(0, 1))
        put(None, line(g, 2, 1), rl.at[g, 1], k_rls.at[g, 1], k_rl.at[g, 1], dev(0, 3))
        to_line(g, 1, 1, 0)
        to_line(g, 3, 0, 1)

    def reduce_relay(g):
        for db, o2 in ((0, 1), (1, 3)):
            arrived(rl.at[g, db], k_rl.at[g, db])
            add_to(line(g, o2, db), [rl.at[g, db]])
            to_line(g, o2, db, db)

    def reduce_line(g):
        for db in range(2):
            for side in range(2):
                arrived(r1.at[g, side, db], k_r1.at[g, side, db])
            add_to(line(g, 0, db), [r1.at[g, 0, db], r1.at[g, 1, db]])
        for o1 in (2, 1, 3):
            put(
                None, ob.at[:, g, a2, lax.rem(a1 + o1, 4)], r2.at[g, o1 - 1],
                k_r2s.at[g, o1 - 1], k_r2.at[g, o1 - 1], dev(o1, 0),
            )

    def finish(g):
        for o in range(3):
            arrived(r2.at[g, o], k_r2.at[g, o])
        for db in range(2):
            total = ob[db, g, a2, a1].astype(f32)
            for o in range(3):
                total = total + r2[g, o, db].astype(f32)
            fb[g, db] = total.astype(bf16)
        for rel, zz, db in ((1, za, 1 - i), (0, z, i)):
            put(
                (tau == c) if rel == 0 else None, fb.at[g, db], oo.at[c, g],
                k_os.at[g, rel], k_o.at[g, c], at_z(zz, tau),
            )

    def out(g):
        @pl.loop(0, 2)
        def _(db):
            @pl.loop(0, 2)
            def _(j):
                ds = pl.ds(pl.multiple_of(j * 512, 512), 512)
                prod = mm(gv[g].reshape(GROUP, HID), wv[db, ds, :], 1, 1)
                ob[db, g, :, :, :, ds] = prod.astype(bf16).reshape(4, 4, PIECE, 512)

    for g in range(4):
        if g == 0:
            weight_grads(None, (1,))
        arrived(pr.at[late(g)], k_b2.at[g])
        combine(g)
        if g == 0:
            weight_grads(None, (0,))
        else:
            weight_grads(g - 1)
            reduce_relay(g - 1)
        if g > 1:
            reduce_line(g - 2)
        activate(g)
        if g == 3:
            weight_grads(3, (1,))
        out(g)
        reduce_start(g)
    weight_grads(3, (0,))
    reduce_relay(3)
    finish(0)
    reduce_line(2)
    finish(1)
    reduce_line(3)
    finish(2)
    finish(3)

    for role in range(2):
        for g in range(4):
            arrived(oo.at[role, g], k_o.at[g, role])
        for m in range(4):
            for rel, out in ((0, ga), (1, gb)):
                for part in range(2):
                    arrived(
                        out.at[role, pl.ds(part * 512, 512), pl.ds(m * UNIT, UNIT)], k_g.at[m, rel, role, part]
                    )
    for local, copy in sends:
        if local is None:
            copy.wait_send()
        else:
            @pl.when(jnp.logical_not(local))
            def _():
                copy.wait_send()


def finish_kernel(scale, oo, ga, gb, out, ig, up, down):
    ig[...] = oo[0]
    out[...] = oo[1]
    up[...] = scale * (ga[0].astype(f32) + gb[0].astype(f32))
    down[...] = scale * (ga[1].astype(f32) + gb[1].astype(f32))


def body(tokens, w_up, w_down, cotangent):
    batch_total = tokens.shape[0] * lax.axis_size("col") * lax.axis_size("dp")
    grad_scale = float(batch_total) ** (-0.5)
    dma = pltpu.SemaphoreType.DMA
    anywhere = pl.BlockSpec(memory_space=pl.ANY)
    oo, ga, gb = pl.pallas_call(
        kernel,
        out_shape=(
            jax.ShapeDtypeStruct((2, 4, PIECE, WIDE), bf16),
            jax.ShapeDtypeStruct((2, WIDE, SLICE), bf16),
            jax.ShapeDtypeStruct((2, WIDE, SLICE), bf16),
        ),
        in_specs=[anywhere] * 4,
        out_specs=(anywhere,) * 3,
        scratch_shapes=[
            pltpu.VMEM((2, 4, 4, 4, PIECE, WIDE), bf16),
            pltpu.VMEM((2, WIDE, HID), bf16),
            pltpu.VMEM((4, 4, 4, PIECE, HID), bf16),
            pltpu.VMEM((4, 4, 4, PIECE, HID), bf16),
            pltpu.VMEM((4, 4, 4, PIECE, HID), bf16),
            pltpu.VMEM((4, 4, 4, PIECE, HID), bf16),
            pltpu.VMEM((4, 4, 4, PIECE, HID), bf16),
            pltpu.VMEM((2, 4, 4, 4, PIECE, WIDE), bf16),
            pltpu.VMEM((4, 2, 2, 4, PIECE, WIDE), bf16),
            pltpu.VMEM((4, 2, 4, PIECE, WIDE), bf16),
            pltpu.VMEM((4, 3, 2, PIECE, WIDE), bf16),
            pltpu.VMEM((4, 2, PIECE, WIDE), bf16),
            pltpu.VMEM((2, WIDE, HID), bf16),
            pltpu.VMEM((2, WIDE, PASSES[1][1]), f32),
            dma((2,)), dma((2, 16)),
            dma((4, 2, 2)), dma((8, 2)),
            dma((30,)),
            dma((2, 16)), dma((2, 16)), dma((4,)), dma((4,)),
            dma((16,)), dma((16,)), dma((4, 4)), dma((4, 4)),
            dma((4, 2, 2)), dma((4, 2, 2)), dma((4, 2)), dma((4, 2)),
            dma((4, 3)), dma((4, 3)),
            dma((8, 2, 2)), dma((4, 2, 2, 2)),
            dma((4, 2)), dma((4, 2)),
        ],
        compiler_params=pltpu.CompilerParams(
            collective_id=0, has_side_effects=True, vmem_limit_bytes=63 << 20
        ),
        name="ffn",
    )(tokens.reshape(4, PIECE, WIDE), cotangent.reshape(4, PIECE, WIDE), w_up, w_down)
    oo = oo.reshape(2, SHARD, WIDE)
    steps = 4
    rows, wide = WIDE // steps, SHARD // steps
    small, large = pl.BlockSpec((wide, WIDE), lambda k: (k, 0)), pl.BlockSpec((rows, SLICE), lambda k: (k, 0))
    pair = pl.BlockSpec((2, rows, SLICE), lambda k: (0, k, 0))
    token_out = jax.ShapeDtypeStruct((SHARD, WIDE), bf16)
    weight_out = jax.ShapeDtypeStruct((WIDE, SLICE), f32)
    return pl.pallas_call(
        functools.partial(finish_kernel, grad_scale),
        grid=(steps,),
        out_shape=(token_out, token_out, weight_out, weight_out),
        in_specs=[pl.BlockSpec((2, wide, WIDE), lambda k: (0, k, 0)), pair, pair],
        out_specs=(small, small, large, large),
        name="finish",
    )(oo, ga, gb)


def solution(mesh):
    placed = (P(("dp", "col"), "row"), P("row", "col"), P("row", "col"), P(("dp", "col"), "row"))
    return jax.shard_map(
        body,
        mesh=mesh,
        in_specs=placed,
        out_specs=(
            P(("dp", "col"), "row"),
            P(("dp", "col"), "row"),
            P("row", ("col", "dp")),
            P("row", ("col", "dp")),
        ),
        check_vma=False,
    )
```

```python
import functools

import jax
import jax.numpy as jnp
from jax import lax
from jax.experimental import pallas as pl
from jax.experimental.pallas import tpu as pltpu
from jax.sharding import PartitionSpec as P

MESH = pl.DeviceIdType.MESH
bf16 = jnp.bfloat16
f32 = jnp.float32
gelu_coef = 0.7978845608
cubic_coef = 0.044715

SHARD = 128
WIDE = 1024
SLICE = 512
TOK = 16 * SHARD
HID = 2 * SLICE
UNIT = 128
CHUNKS = ((0, 2), (2, 2), (4, 4))
EARLY = 4 * UNIT
PASSES = ((0, EARLY), (EARLY, HID - EARLY))
PIECE = SHARD // 4
GROUP = 16 * PIECE


def mm(left, right, dim_left, dim_right):
    return lax.dot_general(
        left, right, (((dim_left,), (dim_right,)), ((), ())), preferred_element_type=f32
    )


def kernel(
    tok, cot, wup, wdn, oo, ga, gb,
    xv, wv, pb, pr, sb, sr, gv, ob, r1, rl, r2, fb, gs, acc,
    k_xin, k_x, k_ws, k_w, k_ag, k_bs, k_b, k_bs2, k_b2, k_ss, k_s, k_ts, k_t,
    k_r1s, k_r1, k_rls, k_rl, k_r2s, k_r2, k_gs, k_g, k_os, k_o,
):
    dp, z, c = lax.axis_index("dp"), lax.axis_index("row"), lax.axis_index("col")
    y, x = lax.div(dp, 4), lax.rem(dp, 4)
    half, i = lax.div(z, 2), lax.rem(z, 2)
    za, zb = z + 1 - 2 * i, 3 - z
    tau = lax.rem(lax.div(z + 1, 2), 2)

    def remote(src, dst, send, recv, dev):
        return pltpu.make_async_remote_copy(
            src_ref=src, dst_ref=dst, send_sem=send, recv_sem=recv, device_id=dev, device_id_type=MESH
        )

    def arrived(dst, sem):
        pltpu.make_async_copy(dst, dst, sem).wait()

    a1, a2 = x * (1 - c) + y * c, y * (1 - c) + x * c

    def place(o1, o2):
        return lax.rem(a2 + o2, 4), lax.rem(a1 + o1, 4)

    def number(p):
        return p[0] * 4 + p[1]

    def dev(o1, o2):
        p2, p1 = place(o1, o2)
        return {"dp": (p1 * c + p2 * (1 - c)) * 4 + p1 * (1 - c) + p2 * c, "row": z, "col": c}

    def at_z(zz, cc):
        return {"dp": dp, "row": zz, "col": cc}

    sends = []

    def put(local, src, dst, send, recv, to):
        copy = remote(src, dst, send, recv, to)
        if local is None:
            copy.start()
        else:
            @pl.when(local)
            def _():
                pltpu.make_async_copy(src, dst, recv).start()

            @pl.when(jnp.logical_not(local))
            def _():
                copy.start()
        sends.append((local, copy))

    barrier = pltpu.get_barrier_semaphore()
    peers = [at_z(za, 0), at_z(za, 1), at_z(zb, c), at_z(z, 1 - c)]
    peers += [dev(o, 0) for o in (1, 2, 3)] + [dev(0, o) for o in (1, 2, 3)]
    for peer in peers:
        pl.semaphore_signal(barrier, inc=1, device_id=peer, device_id_type=MESH)
    pl.semaphore_wait(barrier, len(peers))

    own = place(0, 0)
    here = c == tau
    zx = z * (1 - lax.rem(c + tau, 2)) + za * lax.rem(c + tau, 2)
    for role, src, p in ((0, tok, (y, x)), (1, cot, (x, y))):
        put(
            jnp.logical_and(here, c == role), src, xv.at[i, :, p[0], p[1]],
            k_xin.at[role], k_x.at[i, number(p)], at_z(zx, role),
        )
    for m in range(4):
        u = 2 * m + c
        cols = pl.ds(pl.multiple_of(dp * SLICE + m * UNIT, UNIT), UNIT)
        into = pl.ds(pl.multiple_of(u * UNIT, UNIT), UNIT)
        for rel, zz in ((1, za), (0, z)):
            for role, src in ((0, wup), (1, wdn)):
                put(
                    (c == role) if rel == 0 else None, src.at[:, cols], wv.at[i, :, into],
                    k_ws.at[m, rel, role], k_w.at[u, i], at_z(zz, role),
                )

    def weights(k):
        u0, n = CHUNKS[k]
        for u in range(u0, u0 + n):
            for db in range(2):
                arrived(wv.at[db, :, pl.ds(u * UNIT, UNIT)], k_w.at[u, db])

    count = [0]

    def shard_to(db, p, to):
        part = xv.at[db, :, p[0], p[1]]
        put(None, part, part, k_ag.at[count[0]], k_x.at[db, number(p)], to)
        count[0] += 1

    def shard_in(db, p):
        arrived(xv.at[db, :, p[0], p[1]], k_x.at[db, number(p)])

    def hidden(part, m, shape, f0, fw):
        cs = pl.ds(f0, fw)
        total = [mm(xv[(db, *part)].reshape(m, WIDE), wv[db, :, cs], 1, 0) for db in range(2)]
        pb[(*part, slice(None), cs)] = (total[0] + total[1]).astype(bf16).reshape(*shape, PIECE, fw)

    expected = {}

    def hidden_set(shards, first, last):
        n, offsets = shards
        u0, u1 = CHUNKS[first][0], sum(CHUNKS[last])
        f0, fw = u0 * UNIT, (u1 - u0) * UNIT

        @pl.loop(0, n)
        def _(j):
            p = place(*offsets(j))
            hidden((slice(None), p[0], p[1]), SHARD, (4,), f0, fw)

        for j in range(n):
            o = offsets(j)
            p = place(*o)
            at = (slice(None), p[0], p[1], slice(None), pl.ds(f0, fw))
            sem = k_b.at[first, number(p)]
            put(None, pb.at[at], pr.at[at], k_bs.at[first, number(p)], sem, at_z(zb, c))
            expected.setdefault(o, []).append((at, sem))

    halves = (i, 1 - i)

    def across(o1, o2):
        p = place(o1, o2)
        for way, db in enumerate(halves):
            shard_in(db, p)
            if (o2, way) in ((3, 0), (1, 1)):
                shard_to(db, p, dev(0, 4 - o2))

    centre, beside = (3, lambda j: (0, (j + 3) % 4)), (3, lambda j: (j + 1, 0))
    low, high, across_far = (2, lambda j: (3, 3 - 2 * j)), (2, lambda j: (1, 3 - 2 * j)), (1, lambda j: (0, 2))
    edge = (2, lambda j: (2, 3 - 2 * j))
    corners = [(1, lambda j, o1=o1: (o1, 2)) for o1 in (3, 1, 2)]
    for db in halves:
        shard_in(db, own)
        for to in (dev(1, 0), dev(3, 0), dev(0, 1), dev(0, 3)):
            shard_to(db, own, to)
    for o1 in (3, 1):
        p = place(o1, 0)
        for way, db in enumerate(halves):
            shard_in(db, p)
            if (o1, way) in ((3, 0), (1, 1)):
                shard_to(db, p, dev(4 - o1, 0))
            for to in (dev(0, 1), dev(0, 3)):
                shard_to(db, p, to)
    across(0, 3)
    across(0, 1)
    for db in halves:
        shard_in(db, place(2, 0))
        for to in (dev(0, 1), dev(0, 3)):
            shard_to(db, place(2, 0), to)
    weights(0)
    hidden_set(centre, 0, 0)
    hidden_set(beside, 0, 0)
    across(3, 3)
    across(3, 1)
    hidden_set(low, 0, 0)
    weights(1)
    for shards in (centre, beside, low):
        hidden_set(shards, 1, 1)
    across(1, 3)
    across(1, 1)
    hidden_set(high, 0, 1)
    across(0, 2)
    hidden_set(across_far, 0, 1)
    across(2, 3)
    across(2, 1)
    hidden_set(edge, 0, 1)
    for shards in corners:
        across(*shards[1](0))
        hidden_set(shards, 0, 1)
    weights(2)
    f2, w2 = PASSES[1]

    def late(g):
        return (g, slice(None), slice(None), slice(None), pl.ds(f2, w2))

    for g in range(4):
        hidden((g, slice(None), slice(None)), GROUP, (4, 4), f2, w2)
        put(None, pb.at[late(g)], pr.at[late(g)], k_bs2.at[g], k_b2.at[g], at_z(zb, c))

    def columns(p, body):
        f0, fw = PASSES[p]
        for n0 in range(f0, f0 + fw, UNIT):
            body(pl.ds(n0, UNIT))

    def over_set(shards, body):
        @pl.loop(0, shards[0])
        def _(j):
            p2, p1 = place(*shards[1](j))

            @pl.loop(0, 4)
            def _(g):
                columns(0, lambda cs: body((g, p2, p1, slice(None), cs)))

    def over_group(g, body):
        @pl.loop(0, 4)
        def _(p2):
            @pl.loop(0, 4)
            def _(p1):
                columns(1, lambda cs: body((g, p2, p1, slice(None), cs)))

    def add_pair(at):
        sb[at] = (pb[at].astype(f32) + pr[at].astype(f32)).astype(bf16)

    def grad(at):
        hid, back = sb[at].astype(f32), sr[at].astype(f32)
        square = hid * hid
        t = jnp.tanh(gelu_coef * (hid + cubic_coef * square * hid))
        slope = 0.5 * (1.0 + t) + 0.5 * hid * (1.0 - t * t) * gelu_coef * (1.0 + 3.0 * cubic_coef * square)
        gv[at] = (back * slope).astype(bf16)

    def act(at):
        hid = sr[at].astype(f32)
        t = jnp.tanh(gelu_coef * (hid + cubic_coef * hid * hid * hid))
        gv[at] = (0.5 * hid * (1.0 + t)).astype(bf16)

    def combine_set(shards):
        cs = pl.ds(*PASSES[0])
        places = [shards[1](j) for j in range(shards[0])]
        for o in places:
            for at, sem in expected[o]:
                arrived(pr.at[at], sem)
        over_set(shards, add_pair)
        for o in places:
            p2, p1 = place(*o)
            put(
                None, sb.at[:, p2, p1, :, cs], sr.at[:, p1, p2, :, cs],
                k_ss.at[p2 * 4 + p1], k_s.at[p1 * 4 + p2], at_z(z, 1 - c),
            )

    def activate_sets(sets):
        for shards in sets:
            for j in range(shards[0]):
                p2, p1 = place(*shards[1](j))
                arrived(sr.at[:, p2, p1, :, pl.ds(*PASSES[0])], k_s.at[p2 * 4 + p1])
        for role, body in ((0, grad), (1, act)):

            @pl.when(c == role)
            def _():
                for shards in sets:
                    over_set(shards, body)

    def combine(g):
        over_group(g, add_pair)
        for j in range(4):
            cs = pl.ds(*PASSES[1])
            put(
                None, sb.at[g, :, j, :, cs], sr.at[g, j, :, :, cs],
                k_ts.at[g, j], k_t.at[g, j], at_z(z, 1 - c),
            )

    def activate(g):
        for j in range(4):
            arrived(sr.at[g, j, :, :, pl.ds(*PASSES[1])], k_t.at[g, j])
        for role, body in ((0, grad), (1, act)):

            @pl.when(c == role)
            def _():
                over_group(g, body)

    def grads_out(p, rel, part):
        zz, db, out = ((z, i, ga), (za, 1 - i, gb))[rel]
        r = pl.ds(part * 512, 512)
        for u in range(PASSES[p][0] // UNIT, sum(PASSES[p]) // UNIT):
            m, cc = u // 2, u % 2
            put(
                (c == cc) if rel == 0 else None,
                gs.at[db, r, pl.ds(u * UNIT, UNIT)], out.at[c, r, pl.ds(m * UNIT, UNIT)],
                k_gs.at[u, rel, part], k_g.at[m, rel, c, part], at_z(zz, cc),
            )

    def weight_grads(g, rels=(1, 0)):
        f0, fw = PASSES[0 if g is None else 1]
        cs = pl.ds(f0, fw)
        t, n = (slice(None), TOK) if g is None else (g, GROUP)
        for rel in rels:
            db = (i, 1 - i)[rel]
            for part in range(2):

                @pl.loop(0, 2)
                def _(j):
                    r = pl.ds(pl.multiple_of(part * 512 + j * 256, 256), 256)
                    total = mm(xv[db, t, :, :, :, r].reshape(n, 256), gv[t, :, :, :, cs].reshape(n, fw), 0, 0)
                    if g:
                        total = total + acc[db, r, :]
                    if g is None or g == 3:
                        gs[db, r, cs] = total.astype(bf16)
                    else:
                        acc[db, r, :] = total

                if g is None:
                    grads_out(0, rel, part)
                elif g == 3:
                    grads_out(1, rel, part)

    for shards in (centre, beside, low, high, across_far):
        combine_set(shards)
    block = (9, lambda j: ((j % 3 + 3) % 4, (j // 3 + 3) % 4))
    activate_sets([block, (2, lambda j: (2 * j, 2 - 2 * j))])
    for shards in (edge, *corners):
        combine_set(shards)
    activate_sets([edge, (3, lambda j: ((j + 1) % 4, 2))])

    def add_to(target, others):
        @pl.loop(0, 4)
        def _(t1):
            total = target[t1].astype(f32)
            for other in others:
                total = total + other[t1].astype(f32)
            target[t1] = total.astype(bf16)

    def line(g, o2, db):
        return ob.at[db, g, lax.rem(a2 + o2, 4)]

    def to_line(g, o2, db, side):
        put(
            None, line(g, o2, db), r1.at[g, side, db],
            k_r1s.at[g, side, db], k_r1.at[g, side, db], dev(0, o2),
        )

    def reduce_start(g):
        put(None, line(g, 2, 0), rl.at[g, 0], k_rls.at[g, 0], k_rl.at[g, 0], dev(0, 1))
        put(None, line(g, 2, 1), rl.at[g, 1], k_rls.at[g, 1], k_rl.at[g, 1], dev(0, 3))
        to_line(g, 1, 1, 0)
        to_line(g, 3, 0, 1)

    def reduce_relay(g):
        for db, o2 in ((0, 1), (1, 3)):
            arrived(rl.at[g, db], k_rl.at[g, db])
            add_to(line(g, o2, db), [rl.at[g, db]])
            to_line(g, o2, db, db)

    def reduce_line(g):
        for db in range(2):
            for side in range(2):
                arrived(r1.at[g, side, db], k_r1.at[g, side, db])
            add_to(line(g, 0, db), [r1.at[g, 0, db], r1.at[g, 1, db]])
        for o1 in (2, 1, 3):
            put(
                None, ob.at[:, g, a2, lax.rem(a1 + o1, 4)], r2.at[g, o1 - 1],
                k_r2s.at[g, o1 - 1], k_r2.at[g, o1 - 1], dev(o1, 0),
            )

    def finish(g):
        for o in range(3):
            arrived(r2.at[g, o], k_r2.at[g, o])
        for db in range(2):
            total = ob[db, g, a2, a1].astype(f32)
            for o in range(3):
                total = total + r2[g, o, db].astype(f32)
            fb[g, db] = total.astype(bf16)
        for rel, zz, db in ((1, za, 1 - i), (0, z, i)):
            put(
                (tau == c) if rel == 0 else None, fb.at[g, db], oo.at[c, g],
                k_os.at[g, rel], k_o.at[g, c], at_z(zz, tau),
            )

    def out(g):
        @pl.loop(0, 2)
        def _(db):
            @pl.loop(0, 2)
            def _(j):
                ds = pl.ds(pl.multiple_of(j * 512, 512), 512)
                prod = mm(gv[g].reshape(GROUP, HID), wv[db, ds, :], 1, 1)
                ob[db, g, :, :, :, ds] = prod.astype(bf16).reshape(4, 4, PIECE, 512)

    for g in range(4):
        if g == 0:
            weight_grads(None, (1,))
        else:
            weight_grads(g - 1)
        arrived(pr.at[late(g)], k_b2.at[g])
        combine(g)
        if g == 0:
            weight_grads(None, (0,))
        else:
            reduce_relay(g - 1)
        if g > 1:
            reduce_line(g - 2)
        activate(g)
        if g == 3:
            weight_grads(3, (1,))
        out(g)
        reduce_start(g)
    weight_grads(3, (0,))
    reduce_relay(3)
    finish(0)
    reduce_line(2)
    finish(1)
    reduce_line(3)
    finish(2)
    finish(3)

    for role in range(2):
        for g in range(4):
            arrived(oo.at[role, g], k_o.at[g, role])
        for m in range(4):
            for rel, out in ((0, ga), (1, gb)):
                for part in range(2):
                    arrived(
                        out.at[role, pl.ds(part * 512, 512), pl.ds(m * UNIT, UNIT)], k_g.at[m, rel, role, part]
                    )
    for local, copy in sends:
        if local is None:
            copy.wait_send()
        else:
            @pl.when(jnp.logical_not(local))
            def _():
                copy.wait_send()


def finish_kernel(scale, oo, ga, gb, out, ig, up, down):
    ig[...] = oo[0]
    out[...] = oo[1]
    up[...] = scale * (ga[0].astype(f32) + gb[0].astype(f32))
    down[...] = scale * (ga[1].astype(f32) + gb[1].astype(f32))


def body(tokens, w_up, w_down, cotangent):
    batch_total = tokens.shape[0] * lax.axis_size("col") * lax.axis_size("dp")
    grad_scale = float(batch_total) ** (-0.5)
    dma = pltpu.SemaphoreType.DMA
    anywhere = pl.BlockSpec(memory_space=pl.ANY)
    oo, ga, gb = pl.pallas_call(
        kernel,
        out_shape=(
            jax.ShapeDtypeStruct((2, 4, PIECE, WIDE), bf16),
            jax.ShapeDtypeStruct((2, WIDE, SLICE), bf16),
            jax.ShapeDtypeStruct((2, WIDE, SLICE), bf16),
        ),
        in_specs=[anywhere] * 4,
        out_specs=(anywhere,) * 3,
        scratch_shapes=[
            pltpu.VMEM((2, 4, 4, 4, PIECE, WIDE), bf16),
            pltpu.VMEM((2, WIDE, HID), bf16),
            pltpu.VMEM((4, 4, 4, PIECE, HID), bf16),
            pltpu.VMEM((4, 4, 4, PIECE, HID), bf16),
            pltpu.VMEM((4, 4, 4, PIECE, HID), bf16),
            pltpu.VMEM((4, 4, 4, PIECE, HID), bf16),
            pltpu.VMEM((4, 4, 4, PIECE, HID), bf16),
            pltpu.VMEM((2, 4, 4, 4, PIECE, WIDE), bf16),
            pltpu.VMEM((4, 2, 2, 4, PIECE, WIDE), bf16),
            pltpu.VMEM((4, 2, 4, PIECE, WIDE), bf16),
            pltpu.VMEM((4, 3, 2, PIECE, WIDE), bf16),
            pltpu.VMEM((4, 2, PIECE, WIDE), bf16),
            pltpu.VMEM((2, WIDE, HID), bf16),
            pltpu.VMEM((2, WIDE, PASSES[1][1]), f32),
            dma((2,)), dma((2, 16)),
            dma((4, 2, 2)), dma((8, 2)),
            dma((30,)),
            dma((2, 16)), dma((2, 16)), dma((4,)), dma((4,)),
            dma((16,)), dma((16,)), dma((4, 4)), dma((4, 4)),
            dma((4, 2, 2)), dma((4, 2, 2)), dma((4, 2)), dma((4, 2)),
            dma((4, 3)), dma((4, 3)),
            dma((8, 2, 2)), dma((4, 2, 2, 2)),
            dma((4, 2)), dma((4, 2)),
        ],
        compiler_params=pltpu.CompilerParams(
            collective_id=0, has_side_effects=True, vmem_limit_bytes=63 << 20
        ),
        name="ffn",
    )(tokens.reshape(4, PIECE, WIDE), cotangent.reshape(4, PIECE, WIDE), w_up, w_down)
    oo = oo.reshape(2, SHARD, WIDE)
    steps = 2
    rows, wide = WIDE // steps, SHARD // steps
    small, large = pl.BlockSpec((wide, WIDE), lambda k: (k, 0)), pl.BlockSpec((rows, SLICE), lambda k: (k, 0))
    pair = pl.BlockSpec((2, rows, SLICE), lambda k: (0, k, 0))
    token_out = jax.ShapeDtypeStruct((SHARD, WIDE), bf16)
    weight_out = jax.ShapeDtypeStruct((WIDE, SLICE), f32)
    return pl.pallas_call(
        functools.partial(finish_kernel, grad_scale),
        grid=(steps,),
        out_shape=(token_out, token_out, weight_out, weight_out),
        in_specs=[pl.BlockSpec((2, wide, WIDE), lambda k: (0, k, 0)), pair, pair],
        out_specs=(small, small, large, large),
        name="finish",
    )(oo, ga, gb)


def solution(mesh):
    placed = (P(("dp", "col"), "row"), P("row", "col"), P("row", "col"), P(("dp", "col"), "row"))
    return jax.shard_map(
        body,
        mesh=mesh,
        in_specs=placed,
        out_specs=(
            P(("dp", "col"), "row"),
            P(("dp", "col"), "row"),
            P("row", ("col", "dp")),
            P("row", ("col", "dp")),
        ),
        check_vma=False,
    )
```
